256 devices in a mesh: blocks: 32 (over x, z), span: 8 (over y, core).
Axes of the slice: x: 4, y: 4, z: 8, core: 2. Of those that a mesh axis runs over, the one named last changes fastest.
Arguments:
- struct_disp: float32 [3, 131072], P(None, ('blocks', 'span')), may hold values from -3 to 3
- rec_struct: int32 [524288], P(('blocks', 'span')), may hold values from 0 to 511
- rec_block: int32 [524288, 1], P(('blocks', 'span')), may hold values from 0 to 31; in each aligned block of 2048 rows (0 to 2047, 2048 to 4095, ...) at most 128 rows name the same one
- rec_node: int32 [524288], P(('blocks', 'span')), may hold values from 0 to 8191
- rec_weight: float32 [524288], P(('blocks', 'span')), may hold values from 0.2 to 1
- offset: float32 [3, 16, 1024, 2048], P(None, None, 'blocks', 'span'), may hold values from -0.6 to 0.6
- prior_warp: float32 [3, 16, 1024, 2048], P(None, None, 'blocks', 'span'), may hold values from -3 to 3
- inv_volume: float32 [16, 1024, 2048], P(None, 'blocks', 'span'), may hold values from 0.04 to 0.16
- coord_cot: float32 [3, 16, 1024, 2048], P(None, None, 'blocks', 'span'), may hold values from -6 to 6
- vol_cot: float32 [16, 1024, 2048], P(None, 'blocks', 'span'), may hold values from -6 to 6
Outputs:
- warp_field: float32 [3, 16, 1024, 2048], P(None, None, 'blocks', 'span')
- mesh_adjoint: float32 [3, 16, 1024, 2048], P(None, None, 'blocks', 'span')
- struct_sens: float32 [3, 131072], P(None, ('blocks', 'span'))
The draws below stay inside these ranges and needn't reach their ends.
Inputs may be any that keep to these rules, and one draw needn't show every extreme that they name: `rec_block`: in the rows of one device no fluid group is named by more than 128 records, and on some devices one group is named by exactly 128.
All inputs are finite; a program needn't handle non-finite values.
Results may differ from the reference program's by a relative error of at most 0.00002.
Values sent between devices are 32-bit elements; how exact they have to be, the bound alone decides.
No kernel may reach another device: no remote copies, remote signals or barrier semaphores. Data moves between devices by JAX's collectives and lax.ppermute only.
A program may use at most 128 MiB of HBM per device.

```python
import math
import jax
import jax.numpy as jnp
import numpy as np
from jax import lax

WALL_N = 16
CHORD_DEV = 32
SPAN_DEV = 256
SWEEPS = 4
CAPACITY = 128
SNODE_DEV = 512
GROUPS = 32
SLABS = 8
REC_DEV = 2048
RECORDS = 524288
SNODES = 131072
CHORD = 1024
SPANW = 2048
SURF_DEV = 8192


def with_ends(result, stream_key, smallest, top_value):
    place = [jax.random.randint(jax.random.fold_in(stream_key, axis), (), 0, length) for axis, length in enumerate(result.shape)]
    main_axis = result.shape.index(max(result.shape))
    beside = place[:main_axis] + [(place[main_axis] + 1) % result.shape[main_axis]] + place[main_axis + 1:]
    return result.at[tuple(place)].set(smallest).at[tuple(beside)].set(top_value)


def steps_of(stream_key, dims, split, smallest, high):
    level = 1.0
    for axis_at, blocks in split:
        draws = jax.random.uniform(jax.random.fold_in(jax.random.fold_in(stream_key, 6), axis_at), (blocks,), jnp.float32, smallest / len(split), high / len(split))
        level = level * jnp.repeat(jnp.exp(draws), dims[axis_at] // blocks).reshape((-1,) + (1,) * (len(dims) - 1 - axis_at))
    return level


def assign_block(stream_key, own, number, rows, count, top, bound, skew):
    sequence = jax.random.permutation(stream_key, count)
    heavy_load, ordinary = load_shares(count, rows * top, bound, skew, True), load_shares(count, rows * top, bound, skew, False)
    places = jnp.arange(count)

    def named(tallies, turn):
        used = int((tallies > 0).sum())
        fixed = max(1, used // 4)
        shifted = fixed + (places - fixed + turn * (used - fixed)) % max(1, count - fixed)
        return jnp.zeros((count,), jnp.int32).at[sequence[jnp.where(places < fixed, places, shifted)]].set(jnp.asarray(tallies, jnp.int32))

    tallies = jnp.where(number % 4 == 0, named(heavy_load, number // 4), named(ordinary, number - number // 4 - 1))
    mixed = jax.random.permutation(jax.random.fold_in(own, 3), count)
    donor, taker = mixed[0:count // 2 * 2:2], mixed[1:count // 2 * 2:2]
    margin = jnp.minimum(tallies[donor] - 1, bound - tallies[taker]) // 2
    margin = jnp.where((donor == sequence[0]) | (taker == sequence[0]) | (tallies[taker] == 0), 0, jnp.maximum(margin, 0))
    shifted = jax.random.randint(jax.random.fold_in(own, 4), (count // 2,), 0, 1 << 20) % (margin + 1)
    tallies = tallies.at[donor].add(-shifted).at[taker].add(shifted)
    labels = jnp.searchsorted(jnp.cumsum(tallies), jnp.arange(rows * top), side="right").astype(jnp.int32)
    grid = labels.reshape(top, rows).T
    grid = grid[jax.random.permutation(jax.random.fold_in(own, 1), rows)]
    turn = jax.random.randint(jax.random.fold_in(own, 2), (rows, 1), 0, top)
    return jnp.take_along_axis(grid, (jnp.arange(top)[None, :] + turn) % top, axis=1)


def load_shares(amount, total, most, slope, full):
    weights = [(1 << 20) // math.isqrt(standing ** slope) + 1 for standing in range(1, amount + 1)]
    largest = most if full else min(most, max(-(-total // amount), total * weights[0] // sum(weights)))
    least = 1 if total - largest >= amount - 1 else 0
    given, rest = [largest] + [least] * (amount - 1), total - largest - least * (amount - 1)
    while rest > 0:
        movable = [i for i in range(1, amount) if given[i] < largest] or [i for i in range(1, amount) if given[i] < most]
        whole, remaining = sum([weights[i] for i in movable]), rest
        for i in movable:
            more = min(most - given[i], max(1, remaining * weights[i] // whole), rest)
            given[i] = given[i] + more
            rest = rest - more
    return np.array(given)


def noise(rng, dims, width, most, pieces=(), held_as=jnp.bfloat16):
    entries = jax.random.normal(rng, dims, jnp.float32) * width
    if len(pieces) > 0:
        entries = steps_of(rng, dims, pieces, -0.22, 0.18) * entries
    return jnp.clip(entries, min=-most, max=most).astype(held_as)


def setup_inputs(seed: int = 0) -> dict:
    key_list = jax.random.split(jax.random.key(seed), 11)
    struct_disp = noise(key_list[0], (3, SNODES), 0.5, 3.0, ((1, 256),), jnp.float32)
    rec_struct = with_ends(jax.random.randint(key_list[1], (RECORDS,), 0, SNODE_DEV), jax.random.fold_in(key_list[1], 1), 0, SNODE_DEV - 1).astype(jnp.int32)
    rec_block_keys = jax.random.split(jax.random.fold_in(key_list[2], 1), RECORDS // REC_DEV)
    rec_block_turns = jax.random.permutation(jax.random.fold_in(key_list[2], 3), RECORDS // REC_DEV)
    rec_block = jax.vmap(lambda own, number: assign_block(jax.random.fold_in(key_list[2], 2), own, number, REC_DEV, GROUPS, 1, CAPACITY, 2))(rec_block_keys, rec_block_turns).reshape((RECORDS, 1))
    rec_node = with_ends(jax.random.randint(key_list[3], (RECORDS,), 0, SURF_DEV), jax.random.fold_in(key_list[3], 1), 0, SURF_DEV - 1).astype(jnp.int32)
    rec_weight = jnp.clip(0.2 + 0.8 * jax.random.uniform(key_list[4], (RECORDS,), jnp.float32) ** steps_of(key_list[4], (RECORDS,), ((0, 256),), -0.2, 0.2), 0.2, 1.0)
    offset = noise(key_list[5], (3, WALL_N, CHORD, SPANW), 0.1, 0.6, ((2, 32), (3, 8)), jnp.float32)
    prior_warp = noise(key_list[6], (3, WALL_N, CHORD, SPANW), 0.5, 3.0, ((2, 32), (3, 8)), jnp.float32)
    inv_volume = jnp.clip(jnp.exp(math.log(0.16) - 1.3862944 * jax.random.uniform(key_list[7], (WALL_N, CHORD, SPANW), jnp.float32) ** steps_of(key_list[7], (WALL_N, CHORD, SPANW), ((1, 32), (2, 8)), -0.2, 0.2)), 0.04, 0.16)
    coord_cot = noise(key_list[8], (3, WALL_N, CHORD, SPANW), 1.0, 6.0, ((2, 32), (3, 8)), jnp.float32)
    vol_cot = noise(key_list[9], (WALL_N, CHORD, SPANW), 1.0, 6.0, ((1, 32), (2, 8)), jnp.float32)
    return {"struct_disp": struct_disp, "rec_struct": rec_struct, "rec_block": rec_block, "rec_node": rec_node, "rec_weight": rec_weight, "offset": offset, "prior_warp": prior_warp, "inv_volume": inv_volume, "coord_cot": coord_cot, "vol_cot": vol_cot}


def neighbours(field):
    padded = jnp.pad(field, ((0, 0), (1, 1), (1, 1), (1, 1)))
    summed = padded[:, 1:-1, 2:, 1:-1] + padded[:, 1:-1, :-2, 1:-1] + padded[:, 1:-1, 1:-1, 2:] + padded[:, 1:-1, 1:-1, :-2]
    return summed + padded[:, 2:, 1:-1, 1:-1] + padded[:, :-2, 1:-1, 1:-1]


def cross_of(left, right):
    return jnp.stack([left[1] * right[2] - left[2] * right[1], left[2] * right[0] - left[0] * right[2], left[0] * right[1] - left[1] * right[0]])


def add_unit(field, axis_number):
    return field + jnp.eye(3, dtype=jnp.float32)[axis_number][:, None, None, None]


def lower_of(field, dim_number):
    widths = [(0, 0)] * field.ndim
    widths[dim_number] = (1, 0)
    padded = jnp.pad(field, widths)
    return lax.slice_in_dim(padded, 0, field.shape[dim_number], axis=dim_number)


def reference(struct_disp, rec_struct, rec_block, rec_node, rec_weight, offset, prior_warp, inv_volume, coord_cot, vol_cot):
    owner = jnp.arange(RECORDS, dtype=jnp.int32) // REC_DEV
    slab_index = owner % SLABS
    target = rec_block[:, 0]
    node_j = target * CHORD_DEV + rec_node // SPAN_DEV
    node_k = slab_index * SPAN_DEV + rec_node % SPAN_DEV
    struct_row = owner * SNODE_DEV + rec_struct
    moved_rows = struct_disp[:, struct_row] * rec_weight[None, :]
    surface = jnp.zeros((3, CHORD, SPANW), jnp.float32).at[:, node_j, node_k].add(moved_rows)
    wall_index = jnp.arange(WALL_N)
    interior = (wall_index > 0) & (wall_index < WALL_N - 1)
    relax = jnp.where(interior[:, None, None], inv_volume, 0.0)
    warp_field = prior_warp.at[:, 0].set(surface)
    for sweep_index in range(SWEEPS):
        warp_field = warp_field + relax * (neighbours(warp_field) - 6.0 * warp_field)
    shaped = offset + warp_field
    padded = jnp.pad(shaped, ((0, 0), (0, 0), (0, 1), (0, 1)))
    up_i = jnp.pad(shaped[:, 1:], ((0, 0), (0, 1), (0, 0), (0, 0)))
    edge_i = add_unit(up_i - shaped, 0)
    edge_j = add_unit(padded[:, :, 1:, :-1] - shaped, 1)
    edge_k = add_unit(padded[:, :, :-1, 1:] - shaped, 2)
    inside = (wall_index < WALL_N - 1)[:, None, None] & (jnp.arange(CHORD) < CHORD - 1)[None, :, None] & (jnp.arange(SPANW) < SPANW - 1)[None, None, :]
    weight_cell = jnp.where(inside, vol_cot, 0.0)
    grad_i = weight_cell * cross_of(edge_j, edge_k)
    grad_j = weight_cell * cross_of(edge_k, edge_i)
    grad_k = weight_cell * cross_of(edge_i, edge_j)
    adjoint = coord_cot - grad_i + lower_of(grad_i, 1) - grad_j + lower_of(grad_j, 2) - grad_k + lower_of(grad_k, 3)
    for sweep_index in range(SWEEPS):
        flux = relax * adjoint
        adjoint = adjoint + neighbours(flux) - 6.0 * flux
    sens_wall = adjoint[:, 0]
    struct_sens = jnp.zeros((3, SNODES), jnp.float32).at[:, struct_row].add(rec_weight[None, :] * sens_wall[:, node_j, node_k])
    return warp_field, adjoint, struct_sens
```

```python
import functools

import jax
import jax.numpy as jnp
from jax import lax
from jax.experimental import pallas as pl
from jax.experimental.pallas import tpu as pltpu
from jax.sharding import PartitionSpec as P

SWEEPS = 4
CAPACITY = 128
F32 = jnp.float32
BF16 = jnp.bfloat16
NT = (((1,), (1,)), ((), ()))

NI, NJ, NK = 16, 32, 256
ROWS, LANES = 64, 384
TOP = 16
TILES = tuple(range(1, 7))


def vmem_params(mib):
    return pltpu.CompilerParams(vmem_limit_bytes=mib << 20)


def whole(n):
    return [pl.BlockSpec(memory_space=pltpu.VMEM)] * n


def halves(x):
    hi = x.astype(BF16)
    rest = x - hi.astype(F32)
    mid = rest.astype(BF16)
    lo = (rest - mid.astype(F32)).astype(BF16)
    return hi, mid, lo


def hot(count, row):
    return (lax.broadcasted_iota(jnp.int32, (count, CAPACITY), 0) == row).astype(F32).astype(BF16)


def ends():
    block, slab = lax.axis_index("blocks"), lax.axis_index("span")
    last_block = block == lax.axis_size("blocks") - 1
    last_slab = slab == lax.axis_size("span") - 1
    return block == 0, last_block, slab == 0, last_slab


def unless(flag):
    return jnp.where(flag, 0.0, 1.0).astype(F32)


def pack_kernel(prior, offset, coord, inv, vol, up, dn, rt, lf):
    first_block, last_block, first_slab, last_slab = ends()
    keep_up, keep_dn = unless(last_block), unless(first_block)
    keep_rt, keep_lf = unless(last_slab), unless(first_slab)
    start = 0
    for field in (prior, offset, inv, vol):
        count = field.shape[0]
        up[start : start + count] = field[:, 24:32, :] * keep_up
        dn[start : start + count] = field[:, 0:8, :] * keep_dn
        start += count
    low = lax.broadcasted_iota(jnp.int32, (8, NK), 0) < 4
    for m in range(24):
        other = pltpu.roll(coord[m + 24, 24:32, :], 4, 0)
        up[start + m] = jnp.where(low, other, coord[m, 24:32, :]) * keep_up
        other = pltpu.roll(coord[m + 24, 0:8, :], 4, 0)
        dn[start + m] = jnp.where(low, coord[m, 0:8, :], other) * keep_dn
    start += 24
    for p in range(48):
        up[start + p // 8, p % 8 : p % 8 + 1, :] = prior[p, 23:24, :] * keep_up
        dn[start + p // 8, p % 8 : p % 8 + 1, :] = prior[p, 8:9, :] * keep_dn
    slot = lax.broadcasted_iota(jnp.int32, (NJ, 128), 1) // 16
    base = 0
    for field in (prior, offset, coord, inv, vol):
        groups = field.shape[0] // 8

        def one(g, carry, field=field, base=base):
            right = jnp.zeros((NJ, 128), F32)
            left = jnp.zeros((NJ, 128), F32)
            for q in range(8):
                plane = g * 8 + q
                tail = pltpu.roll(field[plane, :, 128:256], (16 * q + 16) % 128, 1)
                head = pltpu.roll(field[plane, :, 0:128], 16 * q, 1) if q else field[plane, :, 0:128]
                right = jnp.where(slot == q, tail, right)
                left = jnp.where(slot == q, head, left)
            rt[base + g] = right * keep_rt
            lf[base + g] = left * keep_lf
            return carry

        lax.fori_loop(0, groups, one, 0)
        base += groups


def corner_kernel(from_lf, from_rt, up, dn):
    first_block, last_block, _, _ = ends()
    keep_up, keep_dn = unless(last_block), unless(first_block)
    for s, side in enumerate((from_lf, from_rt)):
        b = 28 * s
        up[b : b + 22] = side[:, 24:32, :] * keep_up
        dn[b : b + 22] = side[:, 0:8, :] * keep_dn
        up[b + 22 : b + 28] = side[0:6, 16:24, :] * keep_up
        dn[b + 22 : b + 28] = side[0:6, 8:16, :] * keep_dn


def route_kernel(disp, blk, node, struct, weight, send, slots, table, lhs, rhs):
    first = lax.broadcasted_iota(jnp.int32, (32, 128), 0)
    table[...] = jnp.zeros((16, 128), F32)
    for a in range(4):
        table[4 * a : 4 * a + 3, :] = disp[:, 128 * a : 128 * a + 128]
    parts = jnp.concatenate(halves(table[...]), axis=0)
    earlier = (
        lax.broadcasted_iota(jnp.int32, (128, 128), 0) < lax.broadcasted_iota(jnp.int32, (128, 128), 1)
    ).astype(F32).astype(BF16)
    ones = jnp.ones((128, 128), BF16)
    named = [first == blk[c : c + 1, :] for c in range(16)]
    named = [x.astype(F32) for x in named]
    stacked = jnp.concatenate([x.astype(BF16) for x in named], axis=0)
    before = jnp.dot(stacked, earlier, preferred_element_type=F32)
    totals = jnp.dot(stacked, ones, preferred_element_type=F32)
    running = jnp.zeros((32, 128), F32)
    quarter = lax.broadcasted_iota(jnp.int32, (16, 128), 0) // 4
    for c in range(16):
        at = slice(128 * c, 128 * c + 128)
        rank = jnp.sum(named[c] * (before[32 * c : 32 * c + 32] + running), axis=0, keepdims=True)
        running = running + totals[32 * c : 32 * c + 32]
        rhs[:, at] = hot(128, rank.astype(jnp.int32))
        s = struct[c : c + 1, :]
        high, low = s // 128, s % 128
        got = jnp.dot(parts, hot(128, low), preferred_element_type=F32)
        got = got[0:16] + got[16:32] + got[32:48]
        got = jnp.where(quarter == high, got, 0.0)
        got = got[0:8] + got[8:16]
        got = got[0:4] + got[4:8]
        w = weight[c : c + 1, :]
        moved = halves(got[0:3] * w)
        wparts = halves(w)
        n = node[c : c + 1, :]
        rows = [part[v : v + 1] for v in range(3) for part in moved]
        rows += [(n // 256).astype(F32).astype(BF16), (n % 256).astype(F32).astype(BF16)]
        rows += list(wparts)
        rows += [high.astype(F32).astype(BF16), low.astype(F32).astype(BF16)]
        mine = named[c].astype(BF16)
        for p, row in enumerate(rows):
            lhs[32 * p : 32 * p + 32, at] = mine * row
    out = lax.dot_general(lhs[...], rhs[...], NT, preferred_element_type=F32)
    row = lambda p: out[32 * p : 32 * p + 32]
    payload = [row(3 * v) + row(3 * v + 1) + row(3 * v + 2) for v in range(3)]
    payload.append(row(9) * 256.0 + row(10))
    slots[0] = row(11) + row(12) + row(13)
    slots[1] = row(14) * 128.0 + row(15)
    for p, x in enumerate(payload):
        for g in range(32):
            line = x[g : g + 1]
            send[g, 4 + p : 5 + p, :] = line
            if g < 31:
                send[g + 1, p : p + 1, :] = line
            if g > 0:
                send[g - 1, 8 + p : 9 + p, :] = line
    send[0, 0:4, :] = jnp.zeros((4, 128), F32)
    send[31, 8:12, :] = jnp.zeros((4, 128), F32)


def surface_kernel(got, surf, rt, lf, lhs, rhs, lhs_lo, rhs_lo, lhs_up, rhs_up):
    _, _, first_slab, last_slab = ends()
    for s in range(32):
        at = slice(128 * s, 128 * s + 128)
        for kind, (left, right, count, shift) in enumerate(
            ((lhs_lo, rhs_lo, 16, 16), (lhs, rhs, 32, 0), (lhs_up, rhs_up, 16, 0))
        ):
            n = got[s, 4 * kind + 3 : 4 * kind + 4, :].astype(jnp.int32)
            right[:, at] = hot(256, n % 256)
            rows = hot(count, n // 256 - shift)
            parts = halves(got[s, 4 * kind : 4 * kind + 3, :])
            for v in range(3):
                for h in range(3):
                    line = (3 * v + h) * count
                    left[line : line + count, at] = rows * parts[h][v : v + 1]
    for left, right, count, base in ((lhs_lo, rhs_lo, 16, 0), (lhs, rhs, 32, 16), (lhs_up, rhs_up, 16, 48)):
        out = lax.dot_general(left[...], right[...], NT, preferred_element_type=F32)
        for v in range(3):
            b = 3 * v * count
            surf[v, base : base + count, :] = (
                out[b : b + count] + out[b + count : b + 2 * count] + out[b + 2 * count : b + 3 * count]
            )
    rt[...] = surf[:, :, 128:256] * unless(last_slab)
    lf[...] = surf[:, :, 0:128] * unless(first_slab)


def rolled(x, by):
    by = by % x.shape[-1]
    return pltpu.roll(x, by, x.ndim - 1) if by else x


def main_kernel(
    prior, offset, coord, inv, vol, surf, surf_lf, surf_rt, up, dn, lf, rt, cup, cdn,
    warp_out, adj_out, wall,
    w0, w1, s, a, f0, f1, relax, cell, gi, gj, sems,
):
    copies = []

    def copy(src, dst):
        c = pltpu.make_async_copy(src, dst, sems.at[len(copies)])
        c.start()
        copies.append(c)

    inner = (slice(None), slice(TOP, TOP + NJ), slice(0, NK))
    above = (slice(None), slice(8, 16), slice(0, NK))
    below = (slice(None), slice(48, 56), slice(0, NK))
    for field, ext in ((prior, w0), (inv, relax), (offset, s), (vol, cell), (coord, a)):
        copy(field, ext.at[inner])
    for start, count, ext in ((0, 48, w0), (48, 48, s), (96, 16, relax), (112, 16, cell), (128, 24, a.at[0:24])):
        copy(up.at[start : start + count], ext.at[above])
        copy(dn.at[start : start + count], ext.at[below])

    side = lax.broadcasted_iota(jnp.int32, (8, 128), 1) < 64
    halo = slice(256, 384)
    base = 0
    for ext, deep in ((w0, True), (s, False), (a, False), (relax, False), (cell, False)):
        groups = ext.shape[0] // 8

        def one(g, carry, ext=ext, base=base, deep=deep):
            for q in range(8):
                p = g * 8 + q

                def tile(from_rt, from_lf):
                    return jnp.where(side, rolled(from_rt, -16 * q), rolled(from_lf, 112 - 16 * q))

                for t in range(4):
                    rows = slice(8 * t, 8 * t + 8)
                    ext[p, TOP + 8 * t : TOP + 8 * t + 8, halo] = tile(rt[base + g, rows, :], lf[base + g, rows, :])
                ext[p, 8:16, halo] = tile(cup[28 + base + g], cup[base + g])
                ext[p, 48:56, halo] = tile(cdn[28 + base + g], cdn[base + g])
                if deep:
                    ext[p, 0:8, halo] = tile(cup[50 + g], cup[22 + g])
                    ext[p, 56:64, halo] = tile(cdn[50 + g], cdn[22 + g])
            return carry

        lax.fori_loop(0, groups, one, 0)
        base += groups
    for p in range(48):
        w0[p, 7:8, 0:NK] = up[152 + p // 8, p % 8 : p % 8 + 1, :]
        w0[p, 56:57, 0:NK] = dn[152 + p // 8, p % 8 : p % 8 + 1, :]
    for m in range(24):
        a[m + 24, 8:16, 0:NK] = pltpu.roll(up[128 + m], 4, 0)
        a[m + 24, 48:56, 0:NK] = pltpu.roll(dn[128 + m], 4, 0)
    for c in copies:
        c.wait()
    wide = lax.broadcasted_iota(jnp.int32, (ROWS, 128), 1) < 64
    for v in range(3):
        w0[16 * v, :, 0:NK] = surf[v]
        w0[16 * v, :, halo] = jnp.where(wide, surf_rt[v], surf_lf[v])
        for t in TILES:
            r = slice(8 * t, 8 * t + 8)
            w1[16 * v, r, :] = w0[16 * v, r, :]
            w1[16 * v + 15, r, :] = w0[16 * v + 15, r, :]
        for edge in (7, 56):
            w1[16 * v, edge : edge + 1, :] = w0[16 * v, edge : edge + 1, :]

    _, last_block, _, last_slab = ends()

    @pl.when(last_block)
    def _():
        for i in range(NI):
            cell[i, TOP + NJ - 1 : TOP + NJ, :] = jnp.zeros((1, LANES), F32)

    @pl.when(last_slab)
    def _():
        lane = lax.broadcasted_iota(jnp.int32, (48, 128), 1)
        for i in range(NI):
            cell[i, 8:56, 128:256] = jnp.where(lane == 127, 0.0, cell[i, 8:56, 128:256])

    def around(ref, p, r, lanes=slice(0, LANES)):
        total = ref[p, r.start + 1 : r.stop + 1, :] + ref[p, r.start - 1 : r.stop - 1, :]
        here = ref[p, r, :]
        total = total + rolled(here, -1) + rolled(here, 1)
        return total, here

    def warp_sweep(src, dst, last):
        def plane(i, carry):
            for t in TILES:
                r = slice(8 * t, 8 * t + 8)
                rel = relax[i, r, :]
                for v in range(3):
                    p = 16 * v + i
                    total, here = around(src, p, r)
                    total = total + src[p + 1, r, :] + src[p - 1, r, :]
                    new = here + rel * (total - 6.0 * here)
                    dst[p, r, :] = new
                    if last:
                        s[p, r, :] = s[p, r, :] + new
            return carry

        lax.fori_loop(1, NI - 1, plane, 0)

    warp_sweep(w0, w1, False)
    warp_sweep(w1, w0, False)
    warp_sweep(w0, w1, False)
    warp_sweep(w1, w0, True)
    for v in range(3):
        for p in (16 * v, 16 * v + 15):
            for t in TILES:
                r = slice(8 * t, 8 * t + 8)
                s[p, r, :] = s[p, r, :] + w0[p, r, :]
                gi[v, r, :] = jnp.zeros((8, LANES), F32)
                f0[p, r, :] = jnp.zeros((8, LANES), F32)
                f1[p, r, :] = jnp.zeros((8, LANES), F32)
        gj[v, 0:8, :] = jnp.zeros((8, LANES), F32)
    out = pltpu.make_async_copy(w0.at[inner], warp_out, sems.at[len(copies)])
    out.start()

    def cross(x, y, w):
        return (
            w * (x[1] * y[2] - x[2] * y[1]),
            w * (x[2] * y[0] - x[0] * y[2]),
            w * (x[0] * y[1] - x[1] * y[0]),
        )

    def grad_plane(i, carry):
        for t in TILES:
            r = slice(8 * t, 8 * t + 8)
            w = cell[i, r, :]
            rel = relax[i, r, :]
            ei, ej, ek = [], [], []
            for v in range(3):
                p = 16 * v + i
                here = s[p, r, :]
                ei.append(s[p + 1, r, :] - here)
                ej.append(s[p, 8 * t + 1 : 8 * t + 9, :] - here)
                ek.append(rolled(here, -1) - here)
            ei[0], ej[1], ek[2] = ei[0] + 1.0, ej[1] + 1.0, ek[2] + 1.0
            new_i, new_j, new_k = cross(ej, ek, w), cross(ek, ei, w), cross(ei, ej, w)
            for v in range(3):
                p = 16 * v + i
                gj[v, r, :] = new_j[v]
                value = a[p, r, :] - new_i[v] + gi[v, r, :] - new_j[v]
                value = value + gj[v, 8 * t - 1 : 8 * t + 7, :] - new_k[v] + rolled(new_k[v], 1)
                gi[v, r, :] = new_i[v]
                a[p, r, :] = value
                f0[p, r, :] = jnp.where(i > 0, rel, 0.0) * value
        return carry

    lax.fori_loop(0, NI - 1, grad_plane, 0)
    for v in range(3):
        for t in TILES:
            r = slice(8 * t, 8 * t + 8)
            a[16 * v + 15, r, :] = a[16 * v + 15, r, :] + gi[v, r, :]

    def adjoint_sweep(src, dst, last):
        tiles = TILES[1:-1] if last else TILES
        for v in range(3):
            for t in tiles:
                r = slice(8 * t, 8 * t + 8)
                a[16 * v, r, :] = a[16 * v, r, :] + src[16 * v + 1, r, :]
                a[16 * v + 15, r, :] = a[16 * v + 15, r, :] + src[16 * v + 14, r, :]

        def plane(i, carry):
            for t in tiles:
                r = slice(8 * t, 8 * t + 8)
                rel = relax[i, r, :]
                for v in range(3):
                    p = 16 * v + i
                    total, here = around(src, p, r)
                    total = total + src[p + 1, r, :] + src[p - 1, r, :]
                    new = a[p, r, :] + total - 6.0 * here
                    a[p, r, :] = new
                    if not last:
                        dst[p, r, :] = rel * new
            return carry

        lax.fori_loop(1, NI - 1, plane, 0)

    adjoint_sweep(f0, f1, False)
    adjoint_sweep(f1, f0, False)
    adjoint_sweep(f0, f1, False)
    adjoint_sweep(f1, f0, True)
    out2 = pltpu.make_async_copy(a.at[inner], adj_out, sems.at[len(copies) + 1])
    out2.start()
    for v in range(3):
        wall[v] = a[16 * v, TOP : TOP + NJ, 0:NK]
    out.wait()
    out2.wait()


def reply_kernel(wall, got, reply):
    parts = [h for v in range(3) for h in halves(wall[v])]
    table = jnp.concatenate(parts, axis=0)
    lines = lax.broadcasted_iota(jnp.int32, (32, 128), 0)
    for s in range(32):
        n = got[s, 7:8, :].astype(jnp.int32)
        picked = jnp.dot(table, hot(256, n % 256), preferred_element_type=F32)
        mine = lines == n // 256
        for v in range(3):
            b = 96 * v
            x = picked[b : b + 32] + picked[b + 32 : b + 64] + picked[b + 64 : b + 96]
            reply[s, v : v + 1, :] = jnp.sum(jnp.where(mine, x, 0.0), axis=0, keepdims=True)


def sens_kernel(back, slots, out, lhs, rhs):
    quarter = lax.broadcasted_iota(jnp.int32, (4, 128), 0)
    for g in range(32):
        at = slice(128 * g, 128 * g + 128)
        n = slots[1, g : g + 1, :].astype(jnp.int32)
        high, low = n // 128, n % 128
        rhs[:, at] = hot(128, low)
        value = back[g] * slots[0, g : g + 1, :]
        rows = jnp.concatenate([jnp.where(quarter == high, value[v : v + 1], 0.0) for v in range(3)] + [jnp.zeros((4, 128), F32)], axis=0)
        lhs[:, at] = jnp.concatenate(halves(rows), axis=0)
    total = lax.dot_general(lhs[...], rhs[...], NT, preferred_element_type=F32)
    total = total[0:16] + total[16:32] + total[32:48]
    for v in range(3):
        for q in range(4):
            out[v : v + 1, 128 * q : 128 * q + 128] = total[4 * v + q : 4 * v + q + 1]


def shifted(x, axis, by):
    size = lax.axis_size(axis)
    return lax.ppermute(x, axis, [(i, (i + by) % size) for i in range(size)])


def shape(*dims):
    return jax.ShapeDtypeStruct(dims, F32)


def body(struct_disp, rec_struct, rec_block, rec_node, rec_weight, offset, prior_warp, inv_volume, coord_cot, vol_cot):
    prior = prior_warp.reshape(48, NJ, NK)
    off = offset.reshape(48, NJ, NK)
    coord = coord_cot.reshape(48, NJ, NK)

    up, dn, rt, lf = pl.pallas_call(
        pack_kernel,
        name="pack",
        in_specs=whole(5),
        out_specs=whole(4),
        out_shape=(shape(158, 8, 256), shape(158, 8, 256), shape(22, 32, 128), shape(22, 32, 128)),
        compiler_params=vmem_params(32),
    )(prior, off, coord, inv_volume, vol_cot)
    from_up = shifted(up, "blocks", 1)
    from_dn = shifted(dn, "blocks", -1)
    from_lf = shifted(rt, "span", 1)
    from_rt = shifted(lf, "span", -1)

    send, slots = pl.pallas_call(
        route_kernel,
        name="route",
        in_specs=whole(5),
        out_specs=whole(2),
        out_shape=(shape(32, 12, 128), shape(2, 32, 128)),
        scratch_shapes=[pltpu.VMEM((16, 128), F32), pltpu.VMEM((512, 2048), BF16), pltpu.VMEM((128, 2048), BF16)],
        compiler_params=vmem_params(32),
    )(
        struct_disp,
        rec_block.reshape(16, 128),
        rec_node.reshape(16, 128),
        rec_struct.reshape(16, 128),
        rec_weight.reshape(16, 128),
    )
    got = lax.all_to_all(send, "blocks", split_axis=0, concat_axis=0, tiled=True)

    cup, cdn = pl.pallas_call(
        corner_kernel,
        name="corner",
        in_specs=whole(2),
        out_specs=whole(2),
        out_shape=(shape(56, 8, 128), shape(56, 8, 128)),
        compiler_params=vmem_params(16),
    )(from_lf, from_rt)
    cup = shifted(cup, "blocks", 1)
    cdn = shifted(cdn, "blocks", -1)

    surf, srt, slf = pl.pallas_call(
        surface_kernel,
        name="surface",
        in_specs=whole(1),
        out_specs=whole(3),
        out_shape=(shape(3, 64, 256), shape(3, 64, 128), shape(3, 64, 128)),
        scratch_shapes=[
            pltpu.VMEM((288, 4096), BF16),
            pltpu.VMEM((256, 4096), BF16),
            pltpu.VMEM((144, 4096), BF16),
            pltpu.VMEM((256, 4096), BF16),
            pltpu.VMEM((144, 4096), BF16),
            pltpu.VMEM((256, 4096), BF16),
        ],
        compiler_params=vmem_params(32),
    )(got)
    surf_lf = shifted(srt, "span", 1)
    surf_rt = shifted(slf, "span", -1)

    anywhere = pl.BlockSpec(memory_space=pl.ANY)
    warp_field, adjoint, wall = pl.pallas_call(
        main_kernel,
        name="sweeps",
        in_specs=[anywhere] * 5 + whole(9),
        out_specs=[anywhere] * 2 + whole(1),
        out_shape=(shape(48, NJ, NK), shape(48, NJ, NK), shape(3, NJ, NK)),
        scratch_shapes=[pltpu.VMEM((48, ROWS, LANES), F32)] * 6
        + [pltpu.VMEM((16, ROWS, LANES), F32)] * 2
        + [pltpu.VMEM((3, ROWS, LANES), F32)] * 2
        + [pltpu.SemaphoreType.DMA((17,))],
        compiler_params=vmem_params(52),
    )(prior, off, coord, inv_volume, vol_cot, surf, surf_lf, surf_rt, from_up, from_dn, from_lf, from_rt, cup, cdn)

    reply = pl.pallas_call(
        reply_kernel,
        name="reply",
        in_specs=whole(2),
        out_specs=whole(1)[0],
        out_shape=shape(32, 3, 128),
        compiler_params=vmem_params(16),
    )(wall, got)
    back = lax.all_to_all(reply, "blocks", split_axis=0, concat_axis=0, tiled=True)
    struct_sens = pl.pallas_call(
        sens_kernel,
        name="sens",
        in_specs=whole(2),
        out_specs=whole(1)[0],
        out_shape=shape(3, 512),
        scratch_shapes=[pltpu.VMEM((48, 4096), BF16), pltpu.VMEM((128, 4096), BF16)],
        compiler_params=vmem_params(16),
    )(back, slots)
    return (
        warp_field.reshape(3, NI, NJ, NK),
        adjoint.reshape(3, NI, NJ, NK),
        struct_sens,
    )


def solution(mesh):
    placed = (
        P(None, ("blocks", "span")),
        P(("blocks", "span")),
        P(("blocks", "span"), None),
        P(("blocks", "span")),
        P(("blocks", "span")),
        P(None, None, "blocks", "span"),
        P(None, None, "blocks", "span"),
        P(None, "blocks", "span"),
        P(None, None, "blocks", "span"),
        P(None, "blocks", "span"),
    )
    return jax.shard_map(
        body,
        mesh=mesh,
        in_specs=placed,
        out_specs=(
            P(None, None, "blocks", "span"),
            P(None, None, "blocks", "span"),
            P(None, ("blocks", "span")),
        ),
        check_vma=False,
    )
```

```python
import jax
import jax.numpy as jnp
from jax import lax
from jax.experimental import pallas as pl
from jax.experimental.pallas import tpu as pltpu
from jax.sharding import PartitionSpec as P

SWEEPS = 4
CAPACITY = 128
F32 = jnp.float32
BF16 = jnp.bfloat16
NT = (((1,), (1,)), ((), ()))

NI, NJ, NK = 16, 32, 256
ROWS, LANES = 64, 384
TOP = 16
TILES = tuple(range(1, 7))


def vmem_params(mib):
    return pltpu.CompilerParams(vmem_limit_bytes=mib << 20)


def whole(n):
    return [pl.BlockSpec(memory_space=pltpu.VMEM)] * n


def halves(x):
    hi = x.astype(BF16)
    rest = x - hi.astype(F32)
    mid = rest.astype(BF16)
    lo = (rest - mid.astype(F32)).astype(BF16)
    return hi, mid, lo


def hot(count, row):
    return (lax.broadcasted_iota(jnp.int32, (count, CAPACITY), 0) == row).astype(F32).astype(BF16)


def ends():
    block, slab = lax.axis_index("blocks"), lax.axis_index("span")
    last_block = block == lax.axis_size("blocks") - 1
    last_slab = slab == lax.axis_size("span") - 1
    return block == 0, last_block, slab == 0, last_slab


def unless(flag):
    return jnp.where(flag, 0.0, 1.0).astype(F32)


def rolled(x, by):
    by = by % x.shape[-1]
    return pltpu.roll(x, by, x.ndim - 1) if by else x


def pack_sides(fields, rt, lf, keep_rt, keep_lf):
    slot = lax.broadcasted_iota(jnp.int32, (NJ, 128), 1) // 16
    base = 0
    for field in fields:
        groups = field.shape[0] // 8

        def one(g, carry, field=field, base=base):
            right = jnp.zeros((NJ, 128), F32)
            left = jnp.zeros((NJ, 128), F32)
            for q in range(8):
                plane = g * 8 + q
                right = jnp.where(slot == q, rolled(field[plane, :, 128:256], 16 * q + 16), right)
                left = jnp.where(slot == q, rolled(field[plane, :, 0:128], 16 * q), left)
            rt[base + g] = right * keep_rt
            lf[base + g] = left * keep_lf
            return carry

        lax.fori_loop(0, groups, one, 0)
        base += groups


def load(sems, *pairs):
    copies = [pltpu.make_async_copy(src, dst, sems.at[n]) for n, (src, dst) in enumerate(pairs)]
    for c in copies:
        c.start()
    for c in copies:
        c.wait()


def pack_warp_kernel(prior_hbm, inv_hbm, up, dn, prior, inv, sems):
    first_block, last_block, _, _ = ends()
    load(sems, *[(prior_hbm.at[16 * v : 16 * v + 16], prior.at[16 * v : 16 * v + 16]) for v in range(3)], (inv_hbm, inv))
    keep_up, keep_dn = unless(last_block), unless(first_block)
    for v in range(3):
        up[15 * v : 15 * v + 15] = prior[16 * v + 1 : 16 * v + 16, 24:32, :] * keep_up
        dn[15 * v : 15 * v + 15] = prior[16 * v + 1 : 16 * v + 16, 0:8, :] * keep_dn
    up[45:59] = inv[1:15, 24:32, :] * keep_up
    dn[45:59] = inv[1:15, 0:8, :] * keep_dn
    for n in range(45):
        p = 16 * (n // 15) + n % 15 + 1
        up[59 + n // 8, n % 8 : n % 8 + 1, :] = prior[p, 23:24, :] * keep_up
        dn[59 + n // 8, n % 8 : n % 8 + 1, :] = prior[p, 8:9, :] * keep_dn


def pack_rest_kernel(prior_hbm, inv_hbm, off_hbm, coord_hbm, vol_hbm, rt, lf, up, dn, prior, inv, offset, coord, vol, sems):
    first_block, last_block, first_slab, last_slab = ends()
    keep_up, keep_dn = unless(last_block), unless(first_block)
    pairs = [(inv_hbm, inv), (vol_hbm, vol)]
    for v in range(3):
        at = slice(16 * v, 16 * v + 16)
        pairs += [(prior_hbm.at[at], prior.at[at]), (off_hbm.at[at], offset.at[at]), (coord_hbm.at[at], coord.at[at])]
    load(sems, *pairs)
    pack_sides((prior, inv, offset, coord, vol), rt, lf, unless(last_slab), unless(first_slab))
    start = 0
    for field, count in ((offset, 48), (vol, 15)):
        up[start : start + count] = field[0:count, 24:32, :] * keep_up
        dn[start : start + count] = field[0:count, 0:8, :] * keep_dn
        start += count
    low = lax.broadcasted_iota(jnp.int32, (8, NK), 0) < 4
    for m in range(24):
        other = pltpu.roll(coord[m + 24, 24:32, :], 4, 0)
        up[start + m] = jnp.where(low, other, coord[m, 24:32, :]) * keep_up
        other = pltpu.roll(coord[m + 24, 0:8, :], 4, 0)
        dn[start + m] = jnp.where(low, coord[m, 0:8, :], other) * keep_dn


def corner_kernel(from_lf, from_rt, up, dn):
    first_block, last_block, _, _ = ends()
    keep_up, keep_dn = unless(last_block), unless(first_block)
    for s, side in enumerate((from_lf, from_rt)):
        b = 28 * s
        up[b : b + 22] = side[:, 24:32, :] * keep_up
        dn[b : b + 22] = side[:, 0:8, :] * keep_dn
        up[b + 22 : b + 28] = side[0:6, 16:24, :] * keep_up
        dn[b + 22 : b + 28] = side[0:6, 8:16, :] * keep_dn


def route_kernel(disp, blk, node, struct, weight, send, slots, table, lhs, rhs):
    first = lax.broadcasted_iota(jnp.int32, (32, 128), 0)
    table[...] = jnp.zeros((16, 128), F32)
    for a in range(4):
        table[4 * a : 4 * a + 3, :] = disp[:, 128 * a : 128 * a + 128]
    parts = jnp.concatenate(halves(table[...]), axis=0)
    earlier = (
        lax.broadcasted_iota(jnp.int32, (128, 128), 0) < lax.broadcasted_iota(jnp.int32, (128, 128), 1)
    ).astype(F32).astype(BF16)
    ones = jnp.ones((128, 128), BF16)
    named = [first == blk[c : c + 1, :] for c in range(16)]
    named = [x.astype(F32) for x in named]
    stacked = jnp.concatenate([x.astype(BF16) for x in named], axis=0)
    before = jnp.dot(stacked, earlier, preferred_element_type=F32)
    totals = jnp.dot(stacked, ones, preferred_element_type=F32)
    running = jnp.zeros((32, 128), F32)
    quarter = lax.broadcasted_iota(jnp.int32, (16, 128), 0) // 4
    for c in range(16):
        at = slice(128 * c, 128 * c + 128)
        rank = jnp.sum(named[c] * (before[32 * c : 32 * c + 32] + running), axis=0, keepdims=True)
        running = running + totals[32 * c : 32 * c + 32]
        rhs[:, at] = hot(128, rank.astype(jnp.int32))
        s = struct[c : c + 1, :]
        high, low = s // 128, s % 128
        got = jnp.dot(parts, hot(128, low), preferred_element_type=F32)
        got = got[0:16] + got[16:32] + got[32:48]
        got = jnp.where(quarter == high, got, 0.0)
        got = got[0:8] + got[8:16]
        got = got[0:4] + got[4:8]
        w = weight[c : c + 1, :]
        moved = halves(got[0:3] * w)
        wparts = halves(w)
        n = node[c : c + 1, :]
        rows = [part[v : v + 1] for v in range(3) for part in moved]
        rows += [(n // 256).astype(F32).astype(BF16), (n % 256).astype(F32).astype(BF16)]
        rows += list(wparts)
        rows += [high.astype(F32).astype(BF16), low.astype(F32).astype(BF16)]
        mine = named[c].astype(BF16)
        for p, row in enumerate(rows):
            lhs[32 * p : 32 * p + 32, at] = mine * row
    out = lax.dot_general(lhs[...], rhs[...], NT, preferred_element_type=F32)
    row = lambda p: out[32 * p : 32 * p + 32]
    payload = [row(3 * v) + row(3 * v + 1) + row(3 * v + 2) for v in range(3)]
    payload.append(row(9) * 256.0 + row(10))
    slots[0] = row(11) + row(12) + row(13)
    slots[1] = row(14) * 128.0 + row(15)
    for p, x in enumerate(payload):
        for g in range(32):
            line = x[g : g + 1]
            send[g, 4 + p : 5 + p, :] = line
            if g < 31:
                send[g + 1, p : p + 1, :] = line
            if g > 0:
                send[g - 1, 8 + p : 9 + p, :] = line
    send[0, 0:4, :] = jnp.zeros((4, 128), F32)
    send[31, 8:12, :] = jnp.zeros((4, 128), F32)


def surface_kernel(got, surf, rt, lf, lhs, rhs, lhs_lo, rhs_lo, lhs_up, rhs_up):
    _, _, first_slab, last_slab = ends()
    for s in range(32):
        at = slice(128 * s, 128 * s + 128)
        for kind, (left, right, count, shift) in enumerate(
            ((lhs_lo, rhs_lo, 16, 16), (lhs, rhs, 32, 0), (lhs_up, rhs_up, 16, 0))
        ):
            n = got[s, 4 * kind + 3 : 4 * kind + 4, :].astype(jnp.int32)
            right[:, at] = hot(256, n % 256)
            rows = hot(count, n // 256 - shift)
            parts = halves(got[s, 4 * kind : 4 * kind + 3, :])
            for v in range(3):
                for h in range(3):
                    line = (3 * v + h) * count
                    left[line : line + count, at] = rows * parts[h][v : v + 1]
    for left, right, count, base in ((lhs_lo, rhs_lo, 16, 0), (lhs, rhs, 32, 16), (lhs_up, rhs_up, 16, 48)):
        out = lax.dot_general(left[...], right[...], NT, preferred_element_type=F32)
        for v in range(3):
            b = 3 * v * count
            surf[v, base : base + count, :] = (
                out[b : b + count] + out[b + count : b + 2 * count] + out[b + 2 * count : b + 3 * count]
            )
    rt[...] = surf[:, :, 128:256] * unless(last_slab)
    lf[...] = surf[:, :, 0:128] * unless(first_slab)


def copier(sems):
    copies = []

    def copy(src, dst):
        c = pltpu.make_async_copy(src, dst, sems.at[len(copies)])
        c.start()
        copies.append(c)

    return copies, copy


def bring(copy, field, ext):
    for lt in range(2):
        copy(field.at[:, :, 128 * lt : 128 * lt + 128], ext.at[:, lt, TOP : TOP + NJ, :])


def bring_rims(copy, up, dn, start, ext, first, count):
    for lt in range(2):
        at = slice(128 * lt, 128 * lt + 128)
        copy(up.at[start : start + count, :, at], ext.at[first : first + count, lt, 8:16, :])
        copy(dn.at[start : start + count, :, at], ext.at[first : first + count, lt, 48:56, :])


def bring_sides(exts, base, lf, rt, cup, cdn):
    side = lax.broadcasted_iota(jnp.int32, (8, 128), 1) < 64
    for ext, deep in exts:
        groups = ext.shape[0] // 8

        def one(g, carry, ext=ext, base=base, deep=deep):
            for q in range(8):
                p = g * 8 + q

                def tile(from_rt, from_lf):
                    return jnp.where(side, rolled(from_rt, -16 * q), rolled(from_lf, 112 - 16 * q))

                for t in range(4):
                    rows = slice(8 * t, 8 * t + 8)
                    ext[p, 2, TOP + 8 * t : TOP + 8 * t + 8, :] = tile(rt[base + g, rows, :], lf[base + g, rows, :])
                ext[p, 2, 8:16, :] = tile(cup[28 + base + g], cup[base + g])
                ext[p, 2, 48:56, :] = tile(cdn[28 + base + g], cdn[base + g])
                if deep:
                    ext[p, 2, 0:8, :] = tile(cup[50 + g], cup[22 + g])
                    ext[p, 2, 56:64, :] = tile(cdn[50 + g], cdn[22 + g])
            return carry

        lax.fori_loop(0, groups, one, 0)
        base += groups


def beside(tiles, masks):
    first, last = masks
    out = []
    for n, c in enumerate(tiles):
        before = pltpu.roll(jnp.where(last, tiles[(n + 2) % 3], c), 1, 1)
        after = pltpu.roll(jnp.where(first, tiles[(n + 1) % 3], c), 127, 1)
        out.append(before + after)
    return out


def lane_masks():
    lane = lax.broadcasted_iota(jnp.int32, (8, 128), 1)
    return lane == 0, lane == 127


def warp_kernel(prior, inv, surf, surf_lf, surf_rt, up, dn, lf, rt, cup, cdn, warp_out, w0, relax, w1, sems):
    copies, copy = copier(sems)
    bring(copy, prior, w0)
    bring(copy, inv, relax)
    for v in range(3):
        bring_rims(copy, up, dn, 15 * v, w0, 16 * v + 1, 15)
    bring_rims(copy, up, dn, 45, relax, 1, 14)
    bring_sides(((w0, True), (relax, False)), 0, lf, rt, cup, cdn)
    for n in range(45):
        p = 16 * (n // 15) + n % 15 + 1
        for lt in range(2):
            at = slice(128 * lt, 128 * lt + 128)
            w0[p, lt, 7:8, :] = up[59 + n // 8, n % 8 : n % 8 + 1, at]
            w0[p, lt, 56:57, :] = dn[59 + n // 8, n % 8 : n % 8 + 1, at]
    for c in copies:
        c.wait()
    wide = lax.broadcasted_iota(jnp.int32, (ROWS, 128), 1) < 64
    for v in range(3):
        for lt in range(2):
            w0[16 * v, lt] = surf[v, :, 128 * lt : 128 * lt + 128]
        w0[16 * v, 2] = jnp.where(wide, surf_rt[v], surf_lf[v])
    masks = lane_masks()

    def sweep(src, dst):
        def component(v, carry):
            b = 16 * v
            for t in TILES:
                r, below, above = (slice(8 * t + d, 8 * t + 8 + d) for d in (0, 1, -1))
                prev = [src[b, n, r, :] for n in range(3)]
                cur = [src[b + 1, n, r, :] for n in range(3)]
                for n in range(3):
                    dst[b, n, r, :] = prev[n]
                for i in range(1, NI - 1):
                    p = b + i
                    nxt = [src[p + 1, n, r, :] for n in range(3)]
                    flat = beside(cur, masks)
                    for n in range(3):
                        total = ((src[p, n, below, :] + src[p, n, above, :]) + flat[n]) + (nxt[n] + prev[n])
                        dst[p, n, r, :] = cur[n] + relax[i, n, r, :] * (total - 6.0 * cur[n])
                    prev, cur = cur, nxt
                for n in range(3):
                    dst[b + NI - 1, n, r, :] = cur[n]
            return carry

        lax.fori_loop(0, 3, component, 0)

    sweep(w0, w1)
    sweep(w1, w0)
    sweep(w0, w1)
    sweep(w1, w0)
    copies, copy = copier(sems)
    for lt in range(2):
        copy(w0.at[:, lt, TOP : TOP + NJ, :], warp_out.at[:, :, 128 * lt : 128 * lt + 128])
    for c in copies:
        c.wait()


def cross(x, y, w):
    return (
        w * (x[1] * y[2] - x[2] * y[1]),
        w * (x[2] * y[0] - x[0] * y[2]),
        w * (x[0] * y[1] - x[1] * y[0]),
    )


def adjoint_kernel(
    offset, coord, vol, field, relax, up, dn, lf, rt, cup, cdn, got,
    adj_out, reply,
    s, a, f0, f1, cell, gi, gj, sems,
):
    copies, copy = copier(sems)
    bring(copy, offset, s)
    bring(copy, coord, a)
    bring(copy, vol, cell)
    bring_rims(copy, up, dn, 0, s, 0, 48)
    bring_rims(copy, up, dn, 48, cell, 0, 15)
    bring_rims(copy, up, dn, 63, a, 0, 24)
    bring_sides(((s, False), (a, False), (cell, False)), 8, lf, rt, cup, cdn)
    for m in range(24):
        for lt in range(2):
            at = slice(128 * lt, 128 * lt + 128)
            a[m + 24, lt, 8:16, :] = pltpu.roll(up[63 + m, :, at], 4, 0)
            a[m + 24, lt, 48:56, :] = pltpu.roll(dn[63 + m, :, at], 4, 0)
    for c in copies:
        c.wait()
    _, last_block, _, last_slab = ends()

    @pl.when(last_block)
    def _():
        for i in range(NI):
            for n in range(3):
                cell[i, n, TOP + NJ - 1 : TOP + NJ, :] = jnp.zeros((1, 128), F32)

    @pl.when(last_slab)
    def _():
        lane = lax.broadcasted_iota(jnp.int32, (48, 128), 1)
        for i in range(NI):
            cell[i, 1, 8:56, :] = jnp.where(lane == 127, 0.0, cell[i, 1, 8:56, :])

    def shape_plane(p, carry):
        s[p, :, 8:56, :] = s[p, :, 8:56, :] + field[p, :, 8:56, :]
        return carry

    lax.fori_loop(0, 48, shape_plane, 0)
    gi[...] = jnp.zeros((3, 3, ROWS, 128), F32)
    gj[:, :, 0:8, :] = jnp.zeros((3, 3, 8, 128), F32)
    first, last = masks = lane_masks()

    def grad_plane(i, carry):
        for t in TILES:
            r, below, above = (slice(8 * t + d, 8 * t + 8 + d) for d in (0, 1, -1))
            here = [[s[16 * v + i, n, r, :] for n in range(3)] for v in range(3)]
            along = []
            for n in range(3):
                ei = [s[16 * v + i + 1, n, r, :] - here[v][n] for v in range(3)]
                ej = [s[16 * v + i, n, below, :] - here[v][n] for v in range(3)]
                ek = [
                    pltpu.roll(jnp.where(first, here[v][(n + 1) % 3], here[v][n]), 127, 1) - here[v][n]
                    for v in range(3)
                ]
                ei[0], ej[1], ek[2] = ei[0] + 1.0, ej[1] + 1.0, ek[2] + 1.0
                w = cell[i, n, r, :]
                new_i, new_j, new_k = cross(ej, ek, w), cross(ek, ei, w), cross(ei, ej, w)
                along.append(new_k)
                for v in range(3):
                    p = 16 * v + i
                    gj[v, n, r, :] = new_j[v]
                    value = a[p, n, r, :] - new_i[v] + gi[v, n, r, :] - new_j[v]
                    a[p, n, r, :] = value + gj[v, n, above, :] - new_k[v]
                    gi[v, n, r, :] = new_i[v]
            for n in range(3):
                rel = jnp.where(i > 0, relax[i, n, r, :], 0.0)
                for v in range(3):
                    p = 16 * v + i
                    value = a[p, n, r, :] + pltpu.roll(jnp.where(last, along[(n + 2) % 3][v], along[n][v]), 1, 1)
                    a[p, n, r, :] = value
                    f0[p, n, r, :] = rel * value
        return carry

    lax.fori_loop(0, NI - 1, grad_plane, 0)
    for v in range(3):
        p = 16 * v + NI - 1
        a[p, :, 8:56, :] = a[p, :, 8:56, :] + gi[v, :, 8:56, :]

    def sweep(src, dst, final):
        lanes = range(2) if final else range(3)

        def component(v, carry):
            b = 16 * v
            for t in TILES[1:-1] if final else TILES:
                r, below, above = (slice(8 * t + d, 8 * t + 8 + d) for d in (0, 1, -1))
                prev = None
                cur = [src[b + 1, n, r, :] for n in range(3)]
                for n in lanes:
                    a[b, n, r, :] = a[b, n, r, :] + cur[n]
                for i in range(1, NI - 1):
                    p = b + i
                    nxt = [src[p + 1, n, r, :] for n in range(3)] if i < NI - 2 else None
                    flat = beside(cur, masks)
                    for n in lanes:
                        if prev is None:
                            sides = nxt[n]
                        elif nxt is None:
                            sides = prev[n]
                        else:
                            sides = nxt[n] + prev[n]
                        total = ((src[p, n, below, :] + src[p, n, above, :]) + flat[n]) + sides
                        new = a[p, n, r, :] + (total - 6.0 * cur[n])
                        a[p, n, r, :] = new
                        if not final:
                            dst[p, n, r, :] = relax[i, n, r, :] * new
                    prev, cur = cur, nxt
                for n in lanes:
                    a[b + NI - 1, n, r, :] = a[b + NI - 1, n, r, :] + prev[n]
            return carry

        lax.fori_loop(0, 3, component, 0)

    sweep(f0, f1, False)
    sweep(f1, f0, False)
    sweep(f0, f1, False)
    sweep(f1, f0, True)
    copies, copy = copier(sems)
    for lt in range(2):
        copy(a.at[:, lt, TOP : TOP + NJ, :], adj_out.at[:, :, 128 * lt : 128 * lt + 128])

    wall = [jnp.concatenate([a[16 * v, lt, TOP : TOP + NJ, :] for lt in range(2)], axis=1) for v in range(3)]
    table = jnp.concatenate([h for v in range(3) for h in halves(wall[v])], axis=0)
    lines = lax.broadcasted_iota(jnp.int32, (32, 128), 0)
    for q in range(32):
        n = got[q, 7:8, :].astype(jnp.int32)
        picked = jnp.dot(table, hot(256, n % 256), preferred_element_type=F32)
        mine = lines == n // 256
        for v in range(3):
            b = 96 * v
            x = picked[b : b + 32] + picked[b + 32 : b + 64] + picked[b + 64 : b + 96]
            reply[q, v : v + 1, :] = jnp.sum(jnp.where(mine, x, 0.0), axis=0, keepdims=True)
    for c in copies:
        c.wait()


def sens_kernel(back, slots, out, lhs, rhs):
    quarter = lax.broadcasted_iota(jnp.int32, (4, 128), 0)
    for g in range(32):
        at = slice(128 * g, 128 * g + 128)
        n = slots[1, g : g + 1, :].astype(jnp.int32)
        high, low = n // 128, n % 128
        rhs[:, at] = hot(128, low)
        value = back[g] * slots[0, g : g + 1, :]
        rows = jnp.concatenate([jnp.where(quarter == high, value[v : v + 1], 0.0) for v in range(3)] + [jnp.zeros((4, 128), F32)], axis=0)
        lhs[:, at] = jnp.concatenate(halves(rows), axis=0)
    total = lax.dot_general(lhs[...], rhs[...], NT, preferred_element_type=F32)
    total = total[0:16] + total[16:32] + total[32:48]
    for v in range(3):
        for q in range(4):
            out[v : v + 1, 128 * q : 128 * q + 128] = total[4 * v + q : 4 * v + q + 1]


def shifted(x, axis, by):
    size = lax.axis_size(axis)
    return lax.ppermute(x, axis, [(i, (i + by) % size) for i in range(size)])


def shape(*dims):
    return jax.ShapeDtypeStruct(dims, F32)


def body(struct_disp, rec_struct, rec_block, rec_node, rec_weight, offset, prior_warp, inv_volume, coord_cot, vol_cot):
    prior = prior_warp.reshape(48, NJ, NK)
    off = offset.reshape(48, NJ, NK)
    coord = coord_cot.reshape(48, NJ, NK)

    send, slots = pl.pallas_call(
        route_kernel,
        name="route",
        in_specs=whole(5),
        out_specs=whole(2),
        out_shape=(shape(32, 12, 128), shape(2, 32, 128)),
        scratch_shapes=[pltpu.VMEM((16, 128), F32), pltpu.VMEM((512, 2048), BF16), pltpu.VMEM((128, 2048), BF16)],
        compiler_params=vmem_params(16),
    )(
        struct_disp,
        rec_block.reshape(16, 128),
        rec_node.reshape(16, 128),
        rec_struct.reshape(16, 128),
        rec_weight.reshape(16, 128),
    )
    got = lax.all_to_all(send, "blocks", split_axis=0, concat_axis=0, tiled=True)

    prior, inv_volume, off, coord, vol_cot = (
        pltpu.with_memory_space_constraint(x, pltpu.HBM) for x in (prior, inv_volume, off, coord, vol_cot)
    )
    prior_t, inv_t, off_t, coord_t, vol_t = prior, inv_volume, off, coord, vol_cot
    hbm = pl.BlockSpec(memory_space=pltpu.HBM)
    three, one = pltpu.VMEM((48, NJ, NK), F32), pltpu.VMEM((16, NJ, NK), F32)
    light = pl.CostEstimate(flops=1000, bytes_accessed=1000, transcendentals=0)
    up1, dn1 = pl.pallas_call(
        pack_warp_kernel,
        name="pack_warp",
        in_specs=[hbm] * 2,
        out_specs=whole(2),
        out_shape=(shape(65, 8, 256), shape(65, 8, 256)),
        scratch_shapes=[three, one, pltpu.SemaphoreType.DMA((4,))],
        compiler_params=vmem_params(5),
        cost_estimate=light,
    )(prior_t, inv_t)
    up1 = shifted(up1, "blocks", 1)
    dn1 = shifted(dn1, "blocks", -1)
    rt, lf, up2, dn2 = pl.pallas_call(
        pack_rest_kernel,
        name="pack_rest",
        in_specs=[hbm] * 5,
        out_specs=whole(4),
        out_shape=(shape(22, 32, 128), shape(22, 32, 128), shape(87, 8, 256), shape(87, 8, 256)),
        scratch_shapes=[three, one, three, three, one, pltpu.SemaphoreType.DMA((11,))],
        compiler_params=vmem_params(12),
        cost_estimate=light,
    )(prior_t, inv_t, off_t, coord_t, vol_t)
    from_lf = shifted(rt, "span", 1)
    from_rt = shifted(lf, "span", -1)
    cup, cdn = pl.pallas_call(
        corner_kernel,
        name="corner",
        in_specs=whole(2),
        out_specs=whole(2),
        out_shape=(shape(56, 8, 128), shape(56, 8, 128)),
        compiler_params=vmem_params(4),
        cost_estimate=light,
    )(from_lf, from_rt)
    cup = shifted(cup, "blocks", 1)
    cdn = shifted(cdn, "blocks", -1)
    up2, dn2, up1, dn1 = lax.optimization_barrier((up2, dn2, up1, dn1))
    up2 = shifted(up2, "blocks", 1)
    dn2 = shifted(dn2, "blocks", -1)

    surf, srt, slf = pl.pallas_call(
        surface_kernel,
        name="surface",
        in_specs=whole(1),
        out_specs=whole(3),
        out_shape=(shape(3, 64, 256), shape(3, 64, 128), shape(3, 64, 128)),
        scratch_shapes=[
            pltpu.VMEM((288, 4096), BF16),
            pltpu.VMEM((256, 4096), BF16),
            pltpu.VMEM((144, 4096), BF16),
            pltpu.VMEM((256, 4096), BF16),
            pltpu.VMEM((144, 4096), BF16),
            pltpu.VMEM((256, 4096), BF16),
        ],
        compiler_params=vmem_params(16),
    )(got)
    surf_lf = shifted(srt, "span", 1)
    surf_rt = shifted(slf, "span", -1)

    big = pltpu.VMEM((48, 3, ROWS, 128), F32)
    warp_field, field, relax = pl.pallas_call(
        warp_kernel,
        name="warp",
        in_specs=[hbm] * 2 + whole(9),
        out_specs=[hbm] + whole(2),
        out_shape=(shape(48, NJ, NK), shape(48, 3, ROWS, 128), shape(16, 3, ROWS, 128)),
        scratch_shapes=[big, pltpu.SemaphoreType.DMA((20,))],
        compiler_params=vmem_params(16),
        cost_estimate=pl.CostEstimate(flops=60_000_000, bytes_accessed=20_000_000, transcendentals=0),
    )(prior, inv_volume, surf, surf_lf, surf_rt, up1, dn1, from_lf, from_rt, cup, cdn)
    adjoint, reply = pl.pallas_call(
        adjoint_kernel,
        name="adjoint",
        in_specs=[hbm] * 3 + whole(9),
        out_specs=[hbm] + whole(1),
        out_shape=(shape(48, NJ, NK), shape(32, 3, 128)),
        scratch_shapes=[big] * 4
        + [pltpu.VMEM((16, 3, ROWS, 128), F32)]
        + [pltpu.VMEM((3, 3, ROWS, 128), F32)] * 2
        + [pltpu.SemaphoreType.DMA((18,))],
        compiler_params=vmem_params(25),
        cost_estimate=pl.CostEstimate(flops=60_000_000, bytes_accessed=20_000_000, transcendentals=0),
    )(off, coord, vol_cot, field, relax, up2, dn2, from_lf, from_rt, cup, cdn, got)
    back = lax.all_to_all(reply, "blocks", split_axis=0, concat_axis=0, tiled=True)
    struct_sens = pl.pallas_call(
        sens_kernel,
        name="sens",
        in_specs=whole(2),
        out_specs=whole(1)[0],
        out_shape=shape(3, 512),
        scratch_shapes=[pltpu.VMEM((48, 4096), BF16), pltpu.VMEM((128, 4096), BF16)],
        compiler_params=vmem_params(16),
    )(back, slots)
    return (
        warp_field.reshape(3, NI, NJ, NK),
        adjoint.reshape(3, NI, NJ, NK),
        struct_sens,
    )


def solution(mesh):
    placed = (
        P(None, ("blocks", "span")),
        P(("blocks", "span")),
        P(("blocks", "span"), None),
        P(("blocks", "span")),
        P(("blocks", "span")),
        P(None, None, "blocks", "span"),
        P(None, None, "blocks", "span"),
        P(None, "blocks", "span"),
        P(None, None, "blocks", "span"),
        P(None, "blocks", "span"),
    )
    return jax.shard_map(
        body,
        mesh=mesh,
        in_specs=placed,
        out_specs=(
            P(None, None, "blocks", "span"),
            P(None, None, "blocks", "span"),
            P(None, ("blocks", "span")),
        ),
        check_vma=False,
    )
```

```python
import jax
import jax.numpy as jnp
from jax import lax
from jax.experimental import pallas as pl
from jax.experimental.pallas import tpu as pltpu
from jax.sharding import PartitionSpec as P

SWEEPS = 4
CAPACITY = 128
F32 = jnp.float32
BF16 = jnp.bfloat16
NT = (((1,), (1,)), ((), ()))

NI, NJ, NK = 16, 32, 256
ROWS, LANES = 64, 384
TOP = 16
TILES = tuple(range(1, 7))


def vmem_params(mib):
    return pltpu.CompilerParams(vmem_limit_bytes=mib << 20)


def whole(n):
    return [pl.BlockSpec(memory_space=pltpu.VMEM)] * n


def halves(x):
    hi = x.astype(BF16)
    rest = x - hi.astype(F32)
    mid = rest.astype(BF16)
    lo = (rest - mid.astype(F32)).astype(BF16)
    return hi, mid, lo


def hot(count, row):
    return (lax.broadcasted_iota(jnp.int32, (count, CAPACITY), 0) == row).astype(F32).astype(BF16)


def ends():
    block, slab = lax.axis_index("blocks"), lax.axis_index("span")
    last_block = block == lax.axis_size("blocks") - 1
    last_slab = slab == lax.axis_size("span") - 1
    return block == 0, last_block, slab == 0, last_slab


def unless(flag):
    return jnp.where(flag, 0.0, 1.0).astype(F32)


def rolled(x, by):
    by = by % x.shape[-1]
    return pltpu.roll(x, by, x.ndim - 1) if by else x


def pack_sides(field, base, rt, lf, keep_rt, keep_lf):
    slot = lax.broadcasted_iota(jnp.int32, (NJ, 128), 1) // 16
    groups = field.shape[0] // 8

    def one(g, carry):
        right = jnp.zeros((NJ, 128), F32)
        left = jnp.zeros((NJ, 128), F32)
        for q in range(8):
            plane = g * 8 + q
            right = jnp.where(slot == q, rolled(field[plane, :, 128:256], 16 * q + 16), right)
            left = jnp.where(slot == q, rolled(field[plane, :, 0:128], 16 * q), left)
        rt[base + g] = right * keep_rt
        lf[base + g] = left * keep_lf
        return carry

    lax.fori_loop(0, groups, one, 0)
    return base + groups


def load(sems, *pairs):
    copies = [pltpu.make_async_copy(src, dst, sems.at[n]) for n, (src, dst) in enumerate(pairs)]
    for c in copies:
        c.start()
    for c in copies:
        c.wait()


def pack_warp_kernel(prior_hbm, inv_hbm, up, dn, prior, inv, sems):
    first_block, last_block, _, _ = ends()
    load(sems, *[(prior_hbm.at[16 * v : 16 * v + 16], prior.at[16 * v : 16 * v + 16]) for v in range(3)], (inv_hbm, inv))
    keep_up, keep_dn = unless(last_block), unless(first_block)
    for v in range(3):
        up[15 * v : 15 * v + 15] = prior[16 * v + 1 : 16 * v + 16, 24:32, :] * keep_up
        dn[15 * v : 15 * v + 15] = prior[16 * v + 1 : 16 * v + 16, 0:8, :] * keep_dn
    up[45:59] = inv[1:15, 24:32, :] * keep_up
    dn[45:59] = inv[1:15, 0:8, :] * keep_dn
    for n in range(45):
        p = 16 * (n // 15) + n % 15 + 1
        up[59 + n // 8, n % 8 : n % 8 + 1, :] = prior[p, 23:24, :] * keep_up
        dn[59 + n // 8, n % 8 : n % 8 + 1, :] = prior[p, 8:9, :] * keep_dn


def pack_rest_kernel(prior_hbm, inv_hbm, off_hbm, coord_hbm, vol_hbm, rt, lf, up, dn, prior, inv, offset, coord, vol, sems):
    first_block, last_block, first_slab, last_slab = ends()
    keep_up, keep_dn = unless(last_block), unless(first_block)
    pairs = [(inv_hbm, inv), (vol_hbm, vol)]
    for v in range(3):
        at = slice(16 * v, 16 * v + 16)
        pairs += [(prior_hbm.at[at], prior.at[at]), (off_hbm.at[at], offset.at[at]), (coord_hbm.at[at], coord.at[at])]
    copies = [pltpu.make_async_copy(src, dst, sems.at[n]) for n, (src, dst) in enumerate(pairs)]
    for c in copies:
        c.start()
    base = 0
    for field, waits in ((prior, (2, 5, 8)), (inv, (0,)), (offset, (3, 6, 9)), (coord, (4, 7, 10)), (vol, (1,))):
        for n in waits:
            copies[n].wait()
        base = pack_sides(field, base, rt, lf, unless(last_slab), unless(first_slab))
    start = 0
    for field, count in ((offset, 48), (vol, 15)):
        up[start : start + count] = field[0:count, 24:32, :] * keep_up
        dn[start : start + count] = field[0:count, 0:8, :] * keep_dn
        start += count
    low = lax.broadcasted_iota(jnp.int32, (8, NK), 0) < 4
    for m in range(24):
        other = pltpu.roll(coord[m + 24, 24:32, :], 4, 0)
        up[start + m] = jnp.where(low, other, coord[m, 24:32, :]) * keep_up
        other = pltpu.roll(coord[m + 24, 0:8, :], 4, 0)
        dn[start + m] = jnp.where(low, coord[m, 0:8, :], other) * keep_dn


def corner_kernel(from_lf, from_rt, up, dn):
    first_block, last_block, _, _ = ends()
    keep_up, keep_dn = unless(last_block), unless(first_block)
    for s, side in enumerate((from_lf, from_rt)):
        b = 28 * s
        up[b : b + 22] = side[:, 24:32, :] * keep_up
        dn[b : b + 22] = side[:, 0:8, :] * keep_dn
        up[b + 22 : b + 28] = side[0:6, 16:24, :] * keep_up
        dn[b + 22 : b + 28] = side[0:6, 8:16, :] * keep_dn


def route_kernel(disp, blk, node, struct, weight, send, slots, table, lhs, rhs):
    first = lax.broadcasted_iota(jnp.int32, (32, 128), 0)
    table[...] = jnp.zeros((16, 128), F32)
    for a in range(4):
        table[4 * a : 4 * a + 3, :] = disp[:, 128 * a : 128 * a + 128]
    parts = jnp.concatenate(halves(table[...]), axis=0)
    earlier = (
        lax.broadcasted_iota(jnp.int32, (128, 128), 0) < lax.broadcasted_iota(jnp.int32, (128, 128), 1)
    ).astype(F32).astype(BF16)
    ones = jnp.ones((128, 128), BF16)
    named = [first == blk[c : c + 1, :] for c in range(16)]
    named = [x.astype(F32) for x in named]
    stacked = jnp.concatenate([x.astype(BF16) for x in named], axis=0)
    before = jnp.dot(stacked, earlier, preferred_element_type=F32)
    totals = jnp.dot(stacked, ones, preferred_element_type=F32)
    running = jnp.zeros((32, 128), F32)
    quarter = lax.broadcasted_iota(jnp.int32, (16, 128), 0) // 4
    for c in range(16):
        at = slice(128 * c, 128 * c + 128)
        rank = jnp.sum(named[c] * (before[32 * c : 32 * c + 32] + running), axis=0, keepdims=True)
        running = running + totals[32 * c : 32 * c + 32]
        rhs[:, at] = hot(128, rank.astype(jnp.int32))
        s = struct[c : c + 1, :]
        high, low = s // 128, s % 128
        got = jnp.dot(parts, hot(128, low), preferred_element_type=F32)
        got = got[0:16] + got[16:32] + got[32:48]
        got = jnp.where(quarter == high, got, 0.0)
        got = got[0:8] + got[8:16]
        got = got[0:4] + got[4:8]
        w = weight[c : c + 1, :]
        moved = halves(got[0:3] * w)
        wparts = halves(w)
        n = node[c : c + 1, :]
        rows = [part[v : v + 1] for v in range(3) for part in moved]
        rows += [(n // 256).astype(F32).astype(BF16), (n % 256).astype(F32).astype(BF16)]
        rows += list(wparts)
        rows += [high.astype(F32).astype(BF16), low.astype(F32).astype(BF16)]
        mine = named[c].astype(BF16)
        for p, row in enumerate(rows):
            lhs[32 * p : 32 * p + 32, at] = mine * row
    out = lax.dot_general(lhs[...], rhs[...], NT, preferred_element_type=F32)
    row = lambda p: out[32 * p : 32 * p + 32]
    payload = [row(3 * v) + row(3 * v + 1) + row(3 * v + 2) for v in range(3)]
    payload.append(row(9) * 256.0 + row(10))
    slots[0] = row(11) + row(12) + row(13)
    slots[1] = row(14) * 128.0 + row(15)
    for p, x in enumerate(payload):
        for g in range(32):
            line = x[g : g + 1]
            send[g, 4 + p : 5 + p, :] = line
            if g < 31:
                send[g + 1, p : p + 1, :] = line
            if g > 0:
                send[g - 1, 8 + p : 9 + p, :] = line
    send[0, 0:4, :] = jnp.zeros((4, 128), F32)
    send[31, 8:12, :] = jnp.zeros((4, 128), F32)


def surface_kernel(got, surf, rt, lf, lhs, rhs, lhs_lo, rhs_lo, lhs_up, rhs_up):
    _, _, first_slab, last_slab = ends()
    for s in range(32):
        at = slice(128 * s, 128 * s + 128)
        for kind, (left, right, count, shift) in enumerate(
            ((lhs_lo, rhs_lo, 16, 16), (lhs, rhs, 32, 0), (lhs_up, rhs_up, 16, 0))
        ):
            n = got[s, 4 * kind + 3 : 4 * kind + 4, :].astype(jnp.int32)
            right[:, at] = hot(256, n % 256)
            rows = hot(count, n // 256 - shift)
            parts = halves(got[s, 4 * kind : 4 * kind + 3, :])
            for v in range(3):
                for h in range(3):
                    line = (3 * v + h) * count
                    left[line : line + count, at] = rows * parts[h][v : v + 1]
    for left, right, count, base in ((lhs_lo, rhs_lo, 16, 0), (lhs, rhs, 32, 16), (lhs_up, rhs_up, 16, 48)):
        out = lax.dot_general(left[...], right[...], NT, preferred_element_type=F32)
        for v in range(3):
            b = 3 * v * count
            surf[v, base : base + count, :] = (
                out[b : b + count] + out[b + count : b + 2 * count] + out[b + 2 * count : b + 3 * count]
            )
    rt[...] = surf[:, :, 128:256] * unless(last_slab)
    lf[...] = surf[:, :, 0:128] * unless(first_slab)


def copier(sems):
    copies = []

    def copy(src, dst):
        c = pltpu.make_async_copy(src, dst, sems.at[len(copies)])
        c.start()
        copies.append(c)

    return copies, copy


def bring(copy, field, ext):
    for lt in range(2):
        copy(field.at[:, :, 128 * lt : 128 * lt + 128], ext.at[:, lt, TOP : TOP + NJ, :])


def bring_rims(copy, up, dn, start, ext, first, count):
    for lt in range(2):
        at = slice(128 * lt, 128 * lt + 128)
        copy(up.at[start : start + count, :, at], ext.at[first : first + count, lt, 8:16, :])
        copy(dn.at[start : start + count, :, at], ext.at[first : first + count, lt, 48:56, :])


def bring_sides(exts, base, lf, rt, cup, cdn):
    side = lax.broadcasted_iota(jnp.int32, (8, 128), 1) < 64
    for ext, deep in exts:
        groups = ext.shape[0] // 8

        def one(g, carry, ext=ext, base=base, deep=deep):
            for q in range(8):
                p = g * 8 + q

                def tile(from_rt, from_lf):
                    return jnp.where(side, rolled(from_rt, -16 * q), rolled(from_lf, 112 - 16 * q))

                for t in range(4):
                    rows = slice(8 * t, 8 * t + 8)
                    ext[p, 2, TOP + 8 * t : TOP + 8 * t + 8, :] = tile(rt[base + g, rows, :], lf[base + g, rows, :])
                ext[p, 2, 8:16, :] = tile(cup[28 + base + g], cup[base + g])
                ext[p, 2, 48:56, :] = tile(cdn[28 + base + g], cdn[base + g])
                if deep:
                    ext[p, 2, 0:8, :] = tile(cup[50 + g], cup[22 + g])
                    ext[p, 2, 56:64, :] = tile(cdn[50 + g], cdn[22 + g])
            return carry

        lax.fori_loop(0, groups, one, 0)
        base += groups


def beside(tiles, masks):
    first, last = masks
    out = []
    for n, c in enumerate(tiles):
        before = pltpu.roll(jnp.where(last, tiles[(n + 2) % 3], c), 1, 1)
        after = pltpu.roll(jnp.where(first, tiles[(n + 1) % 3], c), 127, 1)
        out.append(before + after)
    return out


def lane_masks():
    lane = lax.broadcasted_iota(jnp.int32, (8, 128), 1)
    return lane == 0, lane == 127


def warp_kernel(prior, inv, surf, surf_lf, surf_rt, up, dn, lf, rt, cup, cdn, warp_out, w0, relax, w1, sems):
    copies, copy = copier(sems)
    bring(copy, prior, w0)
    bring(copy, inv, relax)
    for v in range(3):
        bring_rims(copy, up, dn, 15 * v, w0, 16 * v + 1, 15)
    bring_rims(copy, up, dn, 45, relax, 1, 14)
    bring_sides(((w0, True), (relax, False)), 0, lf, rt, cup, cdn)
    for n in range(45):
        p = 16 * (n // 15) + n % 15 + 1
        for lt in range(2):
            at = slice(128 * lt, 128 * lt + 128)
            w0[p, lt, 7:8, :] = up[59 + n // 8, n % 8 : n % 8 + 1, at]
            w0[p, lt, 56:57, :] = dn[59 + n // 8, n % 8 : n % 8 + 1, at]
    for c in copies:
        c.wait()
    wide = lax.broadcasted_iota(jnp.int32, (ROWS, 128), 1) < 64
    for v in range(3):
        for lt in range(2):
            w0[16 * v, lt] = surf[v, :, 128 * lt : 128 * lt + 128]
        w0[16 * v, 2] = jnp.where(wide, surf_rt[v], surf_lf[v])
    masks = lane_masks()

    def sweep(src, dst):
        def component(v, carry):
            b = 16 * v
            for t in TILES:
                r, below, above = (slice(8 * t + d, 8 * t + 8 + d) for d in (0, 1, -1))
                prev = [src[b, n, r, :] for n in range(3)]
                cur = [src[b + 1, n, r, :] for n in range(3)]
                for n in range(3):
                    dst[b, n, r, :] = prev[n]
                for i in range(1, NI - 1):
                    p = b + i
                    nxt = [src[p + 1, n, r, :] for n in range(3)]
                    flat = beside(cur, masks)
                    for n in range(3):
                        total = ((src[p, n, below, :] + src[p, n, above, :]) + flat[n]) + (nxt[n] + prev[n])
                        dst[p, n, r, :] = cur[n] + relax[i, n, r, :] * (total - 6.0 * cur[n])
                    prev, cur = cur, nxt
                for n in range(3):
                    dst[b + NI - 1, n, r, :] = cur[n]
            return carry

        lax.fori_loop(0, 3, component, 0)

    sweep(w0, w1)
    sweep(w1, w0)
    sweep(w0, w1)
    sweep(w1, w0)
    copies, copy = copier(sems)
    for lt in range(2):
        copy(w0.at[:, lt, TOP : TOP + NJ, :], warp_out.at[:, :, 128 * lt : 128 * lt + 128])
    for c in copies:
        c.wait()


def cross(x, y, w):
    return (
        w * (x[1] * y[2] - x[2] * y[1]),
        w * (x[2] * y[0] - x[0] * y[2]),
        w * (x[0] * y[1] - x[1] * y[0]),
    )


def adjoint_kernel(
    offset, coord, vol, field, relax, up, dn, lf, rt, cup, cdn, got,
    adj_out, reply,
    s, a, f0, f1, cell, gi, gj, sems,
):
    copies, copy = copier(sems)
    bring(copy, offset, s)
    bring(copy, coord, a)
    bring(copy, vol, cell)
    bring_rims(copy, up, dn, 0, s, 0, 48)
    bring_rims(copy, up, dn, 48, cell, 0, 15)
    bring_rims(copy, up, dn, 63, a, 0, 24)
    bring_sides(((s, False), (a, False), (cell, False)), 8, lf, rt, cup, cdn)
    for m in range(24):
        for lt in range(2):
            at = slice(128 * lt, 128 * lt + 128)
            a[m + 24, lt, 8:16, :] = pltpu.roll(up[63 + m, :, at], 4, 0)
            a[m + 24, lt, 48:56, :] = pltpu.roll(dn[63 + m, :, at], 4, 0)
    for c in copies:
        c.wait()
    _, last_block, _, last_slab = ends()

    @pl.when(last_block)
    def _():
        for i in range(NI):
            for n in range(3):
                cell[i, n, TOP + NJ - 1 : TOP + NJ, :] = jnp.zeros((1, 128), F32)

    @pl.when(last_slab)
    def _():
        lane = lax.broadcasted_iota(jnp.int32, (48, 128), 1)
        for i in range(NI):
            cell[i, 1, 8:56, :] = jnp.where(lane == 127, 0.0, cell[i, 1, 8:56, :])

    def shape_plane(p, carry):
        s[p, :, 8:56, :] = s[p, :, 8:56, :] + field[p, :, 8:56, :]
        return carry

    lax.fori_loop(0, 48, shape_plane, 0)
    gi[...] = jnp.zeros((3, 3, ROWS, 128), F32)
    gj[:, :, 0:8, :] = jnp.zeros((3, 3, 8, 128), F32)
    first, last = masks = lane_masks()

    def grad_plane(i, carry):
        for t in TILES:
            r, below, above = (slice(8 * t + d, 8 * t + 8 + d) for d in (0, 1, -1))
            here = [[s[16 * v + i, n, r, :] for n in range(3)] for v in range(3)]
            along = []
            for n in range(3):
                ei = [s[16 * v + i + 1, n, r, :] - here[v][n] for v in range(3)]
                ej = [s[16 * v + i, n, below, :] - here[v][n] for v in range(3)]
                ek = [
                    pltpu.roll(jnp.where(first, here[v][(n + 1) % 3], here[v][n]), 127, 1) - here[v][n]
                    for v in range(3)
                ]
                ei[0], ej[1], ek[2] = ei[0] + 1.0, ej[1] + 1.0, ek[2] + 1.0
                w = cell[i, n, r, :]
                new_i, new_j, new_k = cross(ej, ek, w), cross(ek, ei, w), cross(ei, ej, w)
                along.append(new_k)
                for v in range(3):
                    p = 16 * v + i
                    gj[v, n, r, :] = new_j[v]
                    value = a[p, n, r, :] - new_i[v] + gi[v, n, r, :] - new_j[v]
                    a[p, n, r, :] = value + gj[v, n, above, :] - new_k[v]
                    gi[v, n, r, :] = new_i[v]
            for n in range(3):
                rel = jnp.where(i > 0, relax[i, n, r, :], 0.0)
                for v in range(3):
                    p = 16 * v + i
                    value = a[p, n, r, :] + pltpu.roll(jnp.where(last, along[(n + 2) % 3][v], along[n][v]), 1, 1)
                    a[p, n, r, :] = value
                    f0[p, n, r, :] = rel * value
        return carry

    lax.fori_loop(0, NI - 1, grad_plane, 0)
    for v in range(3):
        p = 16 * v + NI - 1
        a[p, :, 8:56, :] = a[p, :, 8:56, :] + gi[v, :, 8:56, :]

    def sweep(src, dst, final):
        lanes = range(2) if final else range(3)

        def component(v, carry):
            b = 16 * v
            for t in TILES[1:-1] if final else TILES:
                r, below, above = (slice(8 * t + d, 8 * t + 8 + d) for d in (0, 1, -1))
                prev = None
                cur = [src[b + 1, n, r, :] for n in range(3)]
                for n in lanes:
                    a[b, n, r, :] = a[b, n, r, :] + cur[n]
                for i in range(1, NI - 1):
                    p = b + i
                    nxt = [src[p + 1, n, r, :] for n in range(3)] if i < NI - 2 else None
                    flat = beside(cur, masks)
                    for n in lanes:
                        if prev is None:
                            sides = nxt[n]
                        elif nxt is None:
                            sides = prev[n]
                        else:
                            sides = nxt[n] + prev[n]
                        total = ((src[p, n, below, :] + src[p, n, above, :]) + flat[n]) + sides
                        new = a[p, n, r, :] + (total - 6.0 * cur[n])
                        a[p, n, r, :] = new
                        if not final:
                            dst[p, n, r, :] = relax[i, n, r, :] * new
                    prev, cur = cur, nxt
                for n in lanes:
                    a[b + NI - 1, n, r, :] = a[b + NI - 1, n, r, :] + prev[n]
            return carry

        lax.fori_loop(0, 3, component, 0)

    sweep(f0, f1, False)
    sweep(f1, f0, False)
    sweep(f0, f1, False)
    sweep(f1, f0, True)
    copies, copy = copier(sems)
    for lt in range(2):
        copy(a.at[:, lt, TOP : TOP + NJ, :], adj_out.at[:, :, 128 * lt : 128 * lt + 128])

    wall = [jnp.concatenate([a[16 * v, lt, TOP : TOP + NJ, :] for lt in range(2)], axis=1) for v in range(3)]
    table = jnp.concatenate([h for v in range(3) for h in halves(wall[v])], axis=0)
    lines = lax.broadcasted_iota(jnp.int32, (32, 128), 0)
    for q in range(32):
        n = got[q, 7:8, :].astype(jnp.int32)
        picked = jnp.dot(table, hot(256, n % 256), preferred_element_type=F32)
        mine = lines == n // 256
        for v in range(3):
            b = 96 * v
            x = picked[b : b + 32] + picked[b + 32 : b + 64] + picked[b + 64 : b + 96]
            reply[q, v : v + 1, :] = jnp.sum(jnp.where(mine, x, 0.0), axis=0, keepdims=True)
    for c in copies:
        c.wait()


def sens_kernel(back, slots, out, lhs, rhs):
    quarter = lax.broadcasted_iota(jnp.int32, (4, 128), 0)
    for g in range(32):
        at = slice(128 * g, 128 * g + 128)
        n = slots[1, g : g + 1, :].astype(jnp.int32)
        high, low = n // 128, n % 128
        rhs[:, at] = hot(128, low)
        value = back[g] * slots[0, g : g + 1, :]
        rows = jnp.concatenate([jnp.where(quarter == high, value[v : v + 1], 0.0) for v in range(3)] + [jnp.zeros((4, 128), F32)], axis=0)
        lhs[:, at] = jnp.concatenate(halves(rows), axis=0)
    total = lax.dot_general(lhs[...], rhs[...], NT, preferred_element_type=F32)
    total = total[0:16] + total[16:32] + total[32:48]
    for v in range(3):
        for q in range(4):
            out[v : v + 1, 128 * q : 128 * q + 128] = total[4 * v + q : 4 * v + q + 1]


def shifted(x, axis, by):
    size = lax.axis_size(axis)
    return lax.ppermute(x, axis, [(i, (i + by) % size) for i in range(size)])


def shape(*dims):
    return jax.ShapeDtypeStruct(dims, F32)


def body(struct_disp, rec_struct, rec_block, rec_node, rec_weight, offset, prior_warp, inv_volume, coord_cot, vol_cot):
    prior = prior_warp.reshape(48, NJ, NK)
    off = offset.reshape(48, NJ, NK)
    coord = coord_cot.reshape(48, NJ, NK)

    send, slots = pl.pallas_call(
        route_kernel,
        name="route",
        in_specs=whole(5),
        out_specs=whole(2),
        out_shape=(shape(32, 12, 128), shape(2, 32, 128)),
        scratch_shapes=[pltpu.VMEM((16, 128), F32), pltpu.VMEM((512, 2048), BF16), pltpu.VMEM((128, 2048), BF16)],
        compiler_params=vmem_params(16),
    )(
        struct_disp,
        rec_block.reshape(16, 128),
        rec_node.reshape(16, 128),
        rec_struct.reshape(16, 128),
        rec_weight.reshape(16, 128),
    )
    got = lax.all_to_all(send, "blocks", split_axis=0, concat_axis=0, tiled=True)

    prior, inv_volume, off, coord, vol_cot = (
        pltpu.with_memory_space_constraint(x, pltpu.HBM) for x in (prior, inv_volume, off, coord, vol_cot)
    )
    hbm = pl.BlockSpec(memory_space=pltpu.HBM)
    three, one = pltpu.VMEM((48, NJ, NK), F32), pltpu.VMEM((16, NJ, NK), F32)
    light = pl.CostEstimate(flops=1000, bytes_accessed=1000, transcendentals=0)
    up1, dn1 = pl.pallas_call(
        pack_warp_kernel,
        name="pack_warp",
        in_specs=[hbm] * 2,
        out_specs=whole(2),
        out_shape=(shape(65, 8, 256), shape(65, 8, 256)),
        scratch_shapes=[three, one, pltpu.SemaphoreType.DMA((4,))],
        compiler_params=vmem_params(5),
        cost_estimate=light,
    )(*(pltpu.with_memory_space_constraint(x, pltpu.HBM) for x in lax.optimization_barrier((prior, inv_volume, send))[:2]))
    tied = lax.optimization_barrier((up1, prior, inv_volume, off, coord, vol_cot))[1:]
    prior_t, inv_t, off_t, coord_t, vol_t = (pltpu.with_memory_space_constraint(x, pltpu.HBM) for x in tied)
    up1 = shifted(up1, "blocks", 1)
    dn1 = shifted(dn1, "blocks", -1)
    rt, lf, up2, dn2 = pl.pallas_call(
        pack_rest_kernel,
        name="pack_rest",
        in_specs=[hbm] * 5,
        out_specs=whole(4),
        out_shape=(shape(22, 32, 128), shape(22, 32, 128), shape(87, 8, 256), shape(87, 8, 256)),
        scratch_shapes=[three, one, three, three, one, pltpu.SemaphoreType.DMA((11,))],
        compiler_params=vmem_params(12),
        cost_estimate=light,
    )(prior_t, inv_t, off_t, coord_t, vol_t)
    from_lf = shifted(rt, "span", 1)
    from_rt = shifted(lf, "span", -1)
    cup, cdn = pl.pallas_call(
        corner_kernel,
        name="corner",
        in_specs=whole(2),
        out_specs=whole(2),
        out_shape=(shape(56, 8, 128), shape(56, 8, 128)),
        compiler_params=vmem_params(4),
        cost_estimate=light,
    )(from_lf, from_rt)
    got_t, cup, cdn = lax.optimization_barrier((got, cup, cdn))
    cup = shifted(cup, "blocks", 1)
    cdn = shifted(cdn, "blocks", -1)
    surf, srt, slf = pl.pallas_call(
        surface_kernel,
        name="surface",
        in_specs=whole(1),
        out_specs=whole(3),
        out_shape=(shape(3, 64, 256), shape(3, 64, 128), shape(3, 64, 128)),
        scratch_shapes=[
            pltpu.VMEM((288, 4096), BF16),
            pltpu.VMEM((256, 4096), BF16),
            pltpu.VMEM((144, 4096), BF16),
            pltpu.VMEM((256, 4096), BF16),
            pltpu.VMEM((144, 4096), BF16),
            pltpu.VMEM((256, 4096), BF16),
        ],
        compiler_params=vmem_params(16),
    )(got_t)
    surf_lf = shifted(srt, "span", 1)
    surf_rt = shifted(slf, "span", -1)

    up2, dn2, up1, dn1, cup, cdn, surf_lf, surf_rt = lax.optimization_barrier(
        (up2, dn2, up1, dn1, cup, cdn, surf_lf, surf_rt)
    )
    up2 = shifted(up2, "blocks", 1)
    dn2 = shifted(dn2, "blocks", -1)

    big = pltpu.VMEM((48, 3, ROWS, 128), F32)
    warp_field, field, relax = pl.pallas_call(
        warp_kernel,
        name="warp",
        in_specs=[hbm] * 2 + whole(9),
        out_specs=[hbm] + whole(2),
        out_shape=(shape(48, NJ, NK), shape(48, 3, ROWS, 128), shape(16, 3, ROWS, 128)),
        scratch_shapes=[big, pltpu.SemaphoreType.DMA((20,))],
        compiler_params=vmem_params(16),
        cost_estimate=pl.CostEstimate(flops=60_000_000, bytes_accessed=20_000_000, transcendentals=0),
    )(prior, inv_volume, surf, surf_lf, surf_rt, up1, dn1, from_lf, from_rt, cup, cdn)
    adjoint, reply = pl.pallas_call(
        adjoint_kernel,
        name="adjoint",
        in_specs=[hbm] * 3 + whole(9),
        out_specs=[hbm] + whole(1),
        out_shape=(shape(48, NJ, NK), shape(32, 3, 128)),
        scratch_shapes=[big] * 4
        + [pltpu.VMEM((16, 3, ROWS, 128), F32)]
        + [pltpu.VMEM((3, 3, ROWS, 128), F32)] * 2
        + [pltpu.SemaphoreType.DMA((18,))],
        compiler_params=vmem_params(25),
        cost_estimate=pl.CostEstimate(flops=60_000_000, bytes_accessed=20_000_000, transcendentals=0),
    )(off, coord, vol_cot, field, relax, up2, dn2, from_lf, from_rt, cup, cdn, got)
    back = lax.all_to_all(reply, "blocks", split_axis=0, concat_axis=0, tiled=True)
    struct_sens = pl.pallas_call(
        sens_kernel,
        name="sens",
        in_specs=whole(2),
        out_specs=whole(1)[0],
        out_shape=shape(3, 512),
        scratch_shapes=[pltpu.VMEM((48, 4096), BF16), pltpu.VMEM((128, 4096), BF16)],
        compiler_params=vmem_params(16),
    )(back, slots)
    return (
        warp_field.reshape(3, NI, NJ, NK),
        adjoint.reshape(3, NI, NJ, NK),
        struct_sens,
    )


def solution(mesh):
    placed = (
        P(None, ("blocks", "span")),
        P(("blocks", "span")),
        P(("blocks", "span"), None),
        P(("blocks", "span")),
        P(("blocks", "span")),
        P(None, None, "blocks", "span"),
        P(None, None, "blocks", "span"),
        P(None, "blocks", "span"),
        P(None, None, "blocks", "span"),
        P(None, "blocks", "span"),
    )
    return jax.shard_map(
        body,
        mesh=mesh,
        in_specs=placed,
        out_specs=(
            P(None, None, "blocks", "span"),
            P(None, None, "blocks", "span"),
            P(None, ("blocks", "span")),
        ),
        check_vma=False,
    )
```

```python
import jax
import jax.numpy as jnp
from jax import lax
from jax.experimental import pallas as pl
from jax.experimental.pallas import tpu as pltpu
from jax.sharding import PartitionSpec as P

SWEEPS = 4
CAPACITY = 128
F32 = jnp.float32
BF16 = jnp.bfloat16
NT = (((1,), (1,)), ((), ()))

NI, NJ, NK = 16, 32, 256
ROWS, LANES = 64, 384
TOP = 16
TILES = tuple(range(1, 7))


def vmem_params(mib):
    return pltpu.CompilerParams(vmem_limit_bytes=mib << 20)


def whole(n):
    return [pl.BlockSpec(memory_space=pltpu.VMEM)] * n


def halves(x):
    hi = x.astype(BF16)
    rest = x - hi.astype(F32)
    mid = rest.astype(BF16)
    lo = (rest - mid.astype(F32)).astype(BF16)
    return hi, mid, lo


def hot(count, row):
    return (lax.broadcasted_iota(jnp.int32, (count, CAPACITY), 0) == row).astype(F32).astype(BF16)


def ends():
    block, slab = lax.axis_index("blocks"), lax.axis_index("span")
    last_block = block == lax.axis_size("blocks") - 1
    last_slab = slab == lax.axis_size("span") - 1
    return block == 0, last_block, slab == 0, last_slab


def unless(flag):
    return jnp.where(flag, 0.0, 1.0).astype(F32)


def rolled(x, by):
    by = by % x.shape[-1]
    return pltpu.roll(x, by, x.ndim - 1) if by else x


def pack_sides(field, base, rt, lf, keep_rt, keep_lf):
    slot = lax.broadcasted_iota(jnp.int32, (NJ, 128), 1) // 16
    groups = field.shape[0] // 8

    def one(g, carry):
        right = jnp.zeros((NJ, 128), F32)
        left = jnp.zeros((NJ, 128), F32)
        for q in range(8):
            plane = g * 8 + q
            right = jnp.where(slot == q, rolled(field[plane, :, 128:256], 16 * q + 16), right)
            left = jnp.where(slot == q, rolled(field[plane, :, 0:128], 16 * q), left)
        rt[base + g] = right * keep_rt
        lf[base + g] = left * keep_lf
        return carry

    lax.fori_loop(0, groups, one, 0)
    return base + groups


def load(sems, *pairs):
    copies = [pltpu.make_async_copy(src, dst, sems.at[n]) for n, (src, dst) in enumerate(pairs)]
    for c in copies:
        c.start()
    for c in copies:
        c.wait()


def pack_warp_kernel(prior_hbm, inv_hbm, up, dn, prior, inv, sems):
    first_block, last_block, _, _ = ends()
    load(sems, *[(prior_hbm.at[16 * v : 16 * v + 16], prior.at[16 * v : 16 * v + 16]) for v in range(3)], (inv_hbm, inv))
    keep_up, keep_dn = unless(last_block), unless(first_block)
    for v in range(3):
        up[15 * v : 15 * v + 15] = prior[16 * v + 1 : 16 * v + 16, 24:32, :] * keep_up
        dn[15 * v : 15 * v + 15] = prior[16 * v + 1 : 16 * v + 16, 0:8, :] * keep_dn
    up[45:59] = inv[1:15, 24:32, :] * keep_up
    dn[45:59] = inv[1:15, 0:8, :] * keep_dn
    for n in range(45):
        p = 16 * (n // 15) + n % 15 + 1
        up[59 + n // 8, n % 8 : n % 8 + 1, :] = prior[p, 23:24, :] * keep_up
        dn[59 + n // 8, n % 8 : n % 8 + 1, :] = prior[p, 8:9, :] * keep_dn


def pack_rest_kernel(prior_hbm, inv_hbm, off_hbm, coord_hbm, vol_hbm, rt, lf, up, dn, prior, inv, offset, coord, vol, sems):
    first_block, last_block, first_slab, last_slab = ends()
    keep_up, keep_dn = unless(last_block), unless(first_block)
    pairs = [(inv_hbm, inv), (vol_hbm, vol)]
    for v in range(3):
        at = slice(16 * v, 16 * v + 16)
        pairs += [(prior_hbm.at[at], prior.at[at]), (off_hbm.at[at], offset.at[at]), (coord_hbm.at[at], coord.at[at])]
    copies = [pltpu.make_async_copy(src, dst, sems.at[n]) for n, (src, dst) in enumerate(pairs)]
    for c in copies:
        c.start()
    base = 0
    for field, waits in ((prior, (2, 5, 8)), (inv, (0,)), (offset, (3, 6, 9)), (coord, (4, 7, 10)), (vol, (1,))):
        for n in waits:
            copies[n].wait()
        base = pack_sides(field, base, rt, lf, unless(last_slab), unless(first_slab))
    start = 0
    for field, count in ((offset, 48), (vol, 15)):
        up[start : start + count] = field[0:count, 24:32, :] * keep_up
        dn[start : start + count] = field[0:count, 0:8, :] * keep_dn
        start += count
    low = lax.broadcasted_iota(jnp.int32, (8, NK), 0) < 4
    for m in range(24):
        other = pltpu.roll(coord[m + 24, 24:32, :], 4, 0)
        up[start + m] = jnp.where(low, other, coord[m, 24:32, :]) * keep_up
        other = pltpu.roll(coord[m + 24, 0:8, :], 4, 0)
        dn[start + m] = jnp.where(low, coord[m, 0:8, :], other) * keep_dn


def corner_kernel(from_lf, from_rt, up, dn):
    first_block, last_block, _, _ = ends()
    keep_up, keep_dn = unless(last_block), unless(first_block)
    for s, side in enumerate((from_lf, from_rt)):
        b = 28 * s
        up[b : b + 22] = side[:, 24:32, :] * keep_up
        dn[b : b + 22] = side[:, 0:8, :] * keep_dn
        up[b + 22 : b + 28] = side[0:6, 16:24, :] * keep_up
        dn[b + 22 : b + 28] = side[0:6, 8:16, :] * keep_dn


def route_kernel(
    disp_hbm, blk_hbm, node_hbm, struct_hbm, weight_hbm, send, slots,
    disp, blk, node, struct, weight, table, lhs, rhs, sems,
):
    load(sems, (blk_hbm, blk), (struct_hbm, struct), (disp_hbm, disp), (weight_hbm, weight), (node_hbm, node))
    first = lax.broadcasted_iota(jnp.int32, (32, 128), 0)
    table[...] = jnp.zeros((16, 128), F32)
    for a in range(4):
        table[4 * a : 4 * a + 3, :] = disp[:, 128 * a : 128 * a + 128]
    parts = jnp.concatenate(halves(table[...]), axis=0)
    earlier = (
        lax.broadcasted_iota(jnp.int32, (128, 128), 0) < lax.broadcasted_iota(jnp.int32, (128, 128), 1)
    ).astype(F32).astype(BF16)
    ones = jnp.ones((128, 128), BF16)
    named = [first == blk[c : c + 1, :] for c in range(16)]
    named = [x.astype(F32) for x in named]
    stacked = jnp.concatenate([x.astype(BF16) for x in named], axis=0)
    before = jnp.dot(stacked, earlier, preferred_element_type=F32)
    totals = jnp.dot(stacked, ones, preferred_element_type=F32)
    running = jnp.zeros((32, 128), F32)
    quarter = lax.broadcasted_iota(jnp.int32, (16, 128), 0) // 4
    for c in range(16):
        at = slice(128 * c, 128 * c + 128)
        rank = jnp.sum(named[c] * (before[32 * c : 32 * c + 32] + running), axis=0, keepdims=True)
        running = running + totals[32 * c : 32 * c + 32]
        rhs[:, at] = hot(128, rank.astype(jnp.int32))
        s = struct[c : c + 1, :]
        high, low = s // 128, s % 128
        got = jnp.dot(parts, hot(128, low), preferred_element_type=F32)
        got = got[0:16] + got[16:32] + got[32:48]
        got = jnp.where(quarter == high, got, 0.0)
        got = got[0:8] + got[8:16]
        got = got[0:4] + got[4:8]
        w = weight[c : c + 1, :]
        moved = halves(got[0:3] * w)
        wparts = halves(w)
        n = node[c : c + 1, :]
        rows = [part[v : v + 1] for v in range(3) for part in moved]
        rows += [(n // 256).astype(F32).astype(BF16), (n % 256).astype(F32).astype(BF16)]
        rows += list(wparts)
        rows += [high.astype(F32).astype(BF16), low.astype(F32).astype(BF16)]
        mine = named[c].astype(BF16)
        for p, row in enumerate(rows):
            lhs[32 * p : 32 * p + 32, at] = mine * row
    out = lax.dot_general(lhs[...], rhs[...], NT, preferred_element_type=F32)
    row = lambda p: out[32 * p : 32 * p + 32]
    payload = [row(3 * v) + row(3 * v + 1) + row(3 * v + 2) for v in range(3)]
    payload.append(row(9) * 256.0 + row(10))
    slots[0] = row(11) + row(12) + row(13)
    slots[1] = row(14) * 128.0 + row(15)
    for p, x in enumerate(payload):
        for g in range(32):
            line = x[g : g + 1]
            send[g, 4 + p : 5 + p, :] = line
            if g < 31:
                send[g + 1, p : p + 1, :] = line
            if g > 0:
                send[g - 1, 8 + p : 9 + p, :] = line
    send[0, 0:4, :] = jnp.zeros((4, 128), F32)
    send[31, 8:12, :] = jnp.zeros((4, 128), F32)


def surface_kernel(got, surf, rt, lf, lhs, rhs, lhs_lo, rhs_lo, lhs_up, rhs_up):
    _, _, first_slab, last_slab = ends()
    for s in range(32):
        at = slice(128 * s, 128 * s + 128)
        for kind, (left, right, count, shift) in enumerate(
            ((lhs_lo, rhs_lo, 16, 16), (lhs, rhs, 32, 0), (lhs_up, rhs_up, 16, 0))
        ):
            n = got[s, 4 * kind + 3 : 4 * kind + 4, :].astype(jnp.int32)
            right[:, at] = hot(256, n % 256)
            rows = hot(count, n // 256 - shift)
            parts = halves(got[s, 4 * kind : 4 * kind + 3, :])
            for v in range(3):
                for h in range(3):
                    line = (3 * v + h) * count
                    left[line : line + count, at] = rows * parts[h][v : v + 1]
    for left, right, count, base in ((lhs_lo, rhs_lo, 16, 0), (lhs, rhs, 32, 16), (lhs_up, rhs_up, 16, 48)):
        out = lax.dot_general(left[...], right[...], NT, preferred_element_type=F32)
        for v in range(3):
            b = 3 * v * count
            surf[v, base : base + count, :] = (
                out[b : b + count] + out[b + count : b + 2 * count] + out[b + 2 * count : b + 3 * count]
            )
    rt[...] = surf[:, :, 128:256] * unless(last_slab)
    lf[...] = surf[:, :, 0:128] * unless(first_slab)


def copier(sems):
    copies = []

    def copy(src, dst):
        c = pltpu.make_async_copy(src, dst, sems.at[len(copies)])
        c.start()
        copies.append(c)

    return copies, copy


def bring(copy, field, ext):
    for lt in range(2):
        copy(field.at[:, :, 128 * lt : 128 * lt + 128], ext.at[:, lt, TOP : TOP + NJ, :])


def bring_rims(copy, up, dn, start, ext, first, count):
    for lt in range(2):
        at = slice(128 * lt, 128 * lt + 128)
        copy(up.at[start : start + count, :, at], ext.at[first : first + count, lt, 8:16, :])
        copy(dn.at[start : start + count, :, at], ext.at[first : first + count, lt, 48:56, :])


def bring_sides(exts, base, lf, rt, cup, cdn):
    side = lax.broadcasted_iota(jnp.int32, (8, 128), 1) < 64
    for ext, deep in exts:
        groups = ext.shape[0] // 8

        def one(g, carry, ext=ext, base=base, deep=deep):
            for q in range(8):
                p = g * 8 + q

                def tile(from_rt, from_lf):
                    return jnp.where(side, rolled(from_rt, -16 * q), rolled(from_lf, 112 - 16 * q))

                for t in range(4):
                    rows = slice(8 * t, 8 * t + 8)
                    ext[p, 2, TOP + 8 * t : TOP + 8 * t + 8, :] = tile(rt[base + g, rows, :], lf[base + g, rows, :])
                ext[p, 2, 8:16, :] = tile(cup[28 + base + g], cup[base + g])
                ext[p, 2, 48:56, :] = tile(cdn[28 + base + g], cdn[base + g])
                if deep:
                    ext[p, 2, 0:8, :] = tile(cup[50 + g], cup[22 + g])
                    ext[p, 2, 56:64, :] = tile(cdn[50 + g], cdn[22 + g])
            return carry

        lax.fori_loop(0, groups, one, 0)
        base += groups


def beside(tiles, masks):
    first, last = masks
    out = []
    for n, c in enumerate(tiles):
        before = pltpu.roll(jnp.where(last, tiles[(n + 2) % 3], c), 1, 1)
        after = pltpu.roll(jnp.where(first, tiles[(n + 1) % 3], c), 127, 1)
        out.append(before + after)
    return out


def lane_masks():
    lane = lax.broadcasted_iota(jnp.int32, (8, 128), 1)
    return lane == 0, lane == 127


def warp_kernel(prior, inv, surf, surf_lf, surf_rt, up, dn, lf, rt, cup, cdn, warp_out, w0, relax, w1, sems):
    copies, copy = copier(sems)
    bring(copy, prior, w0)
    bring(copy, inv, relax)
    for v in range(3):
        bring_rims(copy, up, dn, 15 * v, w0, 16 * v + 1, 15)
    bring_rims(copy, up, dn, 45, relax, 1, 14)
    bring_sides(((w0, True), (relax, False)), 0, lf, rt, cup, cdn)
    for n in range(45):
        p = 16 * (n // 15) + n % 15 + 1
        for lt in range(2):
            at = slice(128 * lt, 128 * lt + 128)
            w0[p, lt, 7:8, :] = up[59 + n // 8, n % 8 : n % 8 + 1, at]
            w0[p, lt, 56:57, :] = dn[59 + n // 8, n % 8 : n % 8 + 1, at]
    for c in copies:
        c.wait()
    wide = lax.broadcasted_iota(jnp.int32, (ROWS, 128), 1) < 64
    for v in range(3):
        for lt in range(2):
            w0[16 * v, lt] = surf[v, :, 128 * lt : 128 * lt + 128]
        w0[16 * v, 2] = jnp.where(wide, surf_rt[v], surf_lf[v])
    masks = lane_masks()

    def sweep(src, dst):
        def component(v, carry):
            b = 16 * v
            for t in TILES:
                r, below, above = (slice(8 * t + d, 8 * t + 8 + d) for d in (0, 1, -1))
                prev = [src[b, n, r, :] for n in range(3)]
                cur = [src[b + 1, n, r, :] for n in range(3)]
                for n in range(3):
                    dst[b, n, r, :] = prev[n]
                for i in range(1, NI - 1):
                    p = b + i
                    nxt = [src[p + 1, n, r, :] for n in range(3)]
                    flat = beside(cur, masks)
                    for n in range(3):
                        total = ((src[p, n, below, :] + src[p, n, above, :]) + flat[n]) + (nxt[n] + prev[n])
                        dst[p, n, r, :] = cur[n] + relax[i, n, r, :] * (total - 6.0 * cur[n])
                    prev, cur = cur, nxt
                for n in range(3):
                    dst[b + NI - 1, n, r, :] = cur[n]
            return carry

        lax.fori_loop(0, 3, component, 0)

    sweep(w0, w1)
    sweep(w1, w0)
    sweep(w0, w1)
    sweep(w1, w0)
    copies, copy = copier(sems)
    for lt in range(2):
        copy(w0.at[:, lt, TOP : TOP + NJ, :], warp_out.at[:, :, 128 * lt : 128 * lt + 128])
    for c in copies:
        c.wait()


def cross(x, y, w):
    return (
        w * (x[1] * y[2] - x[2] * y[1]),
        w * (x[2] * y[0] - x[0] * y[2]),
        w * (x[0] * y[1] - x[1] * y[0]),
    )


def adjoint_kernel(
    offset, coord, vol, field, relax, up, dn, lf, rt, cup, cdn, got,
    adj_out, reply,
    s, a, f0, f1, cell, gi, gj, sems,
):
    copies, copy = copier(sems)
    bring(copy, offset, s)
    bring(copy, coord, a)
    bring(copy, vol, cell)
    bring_rims(copy, up, dn, 0, s, 0, 48)
    bring_rims(copy, up, dn, 48, cell, 0, 15)
    bring_rims(copy, up, dn, 63, a, 0, 24)
    bring_sides(((s, False), (a, False), (cell, False)), 8, lf, rt, cup, cdn)
    for m in range(24):
        for lt in range(2):
            at = slice(128 * lt, 128 * lt + 128)
            a[m + 24, lt, 8:16, :] = pltpu.roll(up[63 + m, :, at], 4, 0)
            a[m + 24, lt, 48:56, :] = pltpu.roll(dn[63 + m, :, at], 4, 0)
    for c in copies:
        c.wait()
    _, last_block, _, last_slab = ends()

    @pl.when(last_block)
    def _():
        for i in range(NI):
            for n in range(3):
                cell[i, n, TOP + NJ - 1 : TOP + NJ, :] = jnp.zeros((1, 128), F32)

    @pl.when(last_slab)
    def _():
        lane = lax.broadcasted_iota(jnp.int32, (48, 128), 1)
        for i in range(NI):
            cell[i, 1, 8:56, :] = jnp.where(lane == 127, 0.0, cell[i, 1, 8:56, :])

    def shape_plane(p, carry):
        s[p, :, 8:56, :] = s[p, :, 8:56, :] + field[p, :, 8:56, :]
        return carry

    lax.fori_loop(0, 48, shape_plane, 0)
    gi[...] = jnp.zeros((3, 3, ROWS, 128), F32)
    gj[:, :, 0:8, :] = jnp.zeros((3, 3, 8, 128), F32)
    first, last = masks = lane_masks()

    def grad_plane(i, carry):
        for t in TILES:
            r, below, above = (slice(8 * t + d, 8 * t + 8 + d) for d in (0, 1, -1))
            here = [[s[16 * v + i, n, r, :] for n in range(3)] for v in range(3)]
            along = []
            for n in range(3):
                ei = [s[16 * v + i + 1, n, r, :] - here[v][n] for v in range(3)]
                ej = [s[16 * v + i, n, below, :] - here[v][n] for v in range(3)]
                ek = [
                    pltpu.roll(jnp.where(first, here[v][(n + 1) % 3], here[v][n]), 127, 1) - here[v][n]
                    for v in range(3)
                ]
                ei[0], ej[1], ek[2] = ei[0] + 1.0, ej[1] + 1.0, ek[2] + 1.0
                w = cell[i, n, r, :]
                new_i, new_j, new_k = cross(ej, ek, w), cross(ek, ei, w), cross(ei, ej, w)
                along.append(new_k)
                for v in range(3):
                    p = 16 * v + i
                    gj[v, n, r, :] = new_j[v]
                    value = a[p, n, r, :] - new_i[v] + gi[v, n, r, :] - new_j[v]
                    a[p, n, r, :] = value + gj[v, n, above, :] - new_k[v]
                    gi[v, n, r, :] = new_i[v]
            for n in range(3):
                rel = jnp.where(i > 0, relax[i, n, r, :], 0.0)
                for v in range(3):
                    p = 16 * v + i
                    value = a[p, n, r, :] + pltpu.roll(jnp.where(last, along[(n + 2) % 3][v], along[n][v]), 1, 1)
                    a[p, n, r, :] = value
                    f0[p, n, r, :] = rel * value
        return carry

    lax.fori_loop(0, NI - 1, grad_plane, 0)
    for v in range(3):
        p = 16 * v + NI - 1
        a[p, :, 8:56, :] = a[p, :, 8:56, :] + gi[v, :, 8:56, :]

    def sweep(src, dst, final):
        lanes = range(2) if final else range(3)

        def component(v, carry):
            b = 16 * v
            for t in TILES[1:-1] if final else TILES:
                r, below, above = (slice(8 * t + d, 8 * t + 8 + d) for d in (0, 1, -1))
                prev = None
                cur = [src[b + 1, n, r, :] for n in range(3)]
                for n in lanes:
                    a[b, n, r, :] = a[b, n, r, :] + cur[n]
                for i in range(1, NI - 1):
                    p = b + i
                    nxt = [src[p + 1, n, r, :] for n in range(3)] if i < NI - 2 else None
                    flat = beside(cur, masks)
                    for n in lanes:
                        if prev is None:
                            sides = nxt[n]
                        elif nxt is None:
                            sides = prev[n]
                        else:
                            sides = nxt[n] + prev[n]
                        total = ((src[p, n, below, :] + src[p, n, above, :]) + flat[n]) + sides
                        new = a[p, n, r, :] + (total - 6.0 * cur[n])
                        a[p, n, r, :] = new
                        if not final:
                            dst[p, n, r, :] = relax[i, n, r, :] * new
                    prev, cur = cur, nxt
                for n in lanes:
                    a[b + NI - 1, n, r, :] = a[b + NI - 1, n, r, :] + prev[n]
            return carry

        lax.fori_loop(0, 3, component, 0)

    sweep(f0, f1, False)
    sweep(f1, f0, False)
    sweep(f0, f1, False)
    sweep(f1, f0, True)
    copies, copy = copier(sems)
    for lt in range(2):
        copy(a.at[:, lt, TOP : TOP + NJ, :], adj_out.at[:, :, 128 * lt : 128 * lt + 128])

    wall = [jnp.concatenate([a[16 * v, lt, TOP : TOP + NJ, :] for lt in range(2)], axis=1) for v in range(3)]
    table = jnp.concatenate([h for v in range(3) for h in halves(wall[v])], axis=0)
    lines = lax.broadcasted_iota(jnp.int32, (32, 128), 0)
    for q in range(32):
        n = got[q, 7:8, :].astype(jnp.int32)
        picked = jnp.dot(table, hot(256, n % 256), preferred_element_type=F32)
        mine = lines == n // 256
        for v in range(3):
            b = 96 * v
            x = picked[b : b + 32] + picked[b + 32 : b + 64] + picked[b + 64 : b + 96]
            reply[q, v : v + 1, :] = jnp.sum(jnp.where(mine, x, 0.0), axis=0, keepdims=True)
    for c in copies:
        c.wait()


def sens_kernel(back, slots, out, lhs, rhs):
    quarter = lax.broadcasted_iota(jnp.int32, (4, 128), 0)
    for g in range(32):
        at = slice(128 * g, 128 * g + 128)
        n = slots[1, g : g + 1, :].astype(jnp.int32)
        high, low = n // 128, n % 128
        rhs[:, at] = hot(128, low)
        value = back[g] * slots[0, g : g + 1, :]
        rows = jnp.concatenate([jnp.where(quarter == high, value[v : v + 1], 0.0) for v in range(3)] + [jnp.zeros((4, 128), F32)], axis=0)
        lhs[:, at] = jnp.concatenate(halves(rows), axis=0)
    total = lax.dot_general(lhs[...], rhs[...], NT, preferred_element_type=F32)
    total = total[0:16] + total[16:32] + total[32:48]
    for v in range(3):
        for q in range(4):
            out[v : v + 1, 128 * q : 128 * q + 128] = total[4 * v + q : 4 * v + q + 1]


def shifted(x, axis, by):
    size = lax.axis_size(axis)
    return lax.ppermute(x, axis, [(i, (i + by) % size) for i in range(size)])


def shape(*dims):
    return jax.ShapeDtypeStruct(dims, F32)


def body(struct_disp, rec_struct, rec_block, rec_node, rec_weight, offset, prior_warp, inv_volume, coord_cot, vol_cot):
    prior = prior_warp.reshape(48, NJ, NK)
    off = offset.reshape(48, NJ, NK)
    coord = coord_cot.reshape(48, NJ, NK)

    hbm = pl.BlockSpec(memory_space=pltpu.HBM)
    light = pl.CostEstimate(flops=1000, bytes_accessed=1000, transcendentals=0)
    records = (struct_disp, *(x.reshape(16, 128) for x in (rec_block, rec_node, rec_struct, rec_weight)))
    lines = [pltpu.VMEM((16, 128), dtype) for dtype in (jnp.int32, jnp.int32, jnp.int32, F32)]
    send, slots = pl.pallas_call(
        route_kernel,
        name="route",
        in_specs=[hbm] * 5,
        out_specs=whole(2),
        out_shape=(shape(32, 12, 128), shape(2, 32, 128)),
        scratch_shapes=[pltpu.VMEM((3, 512), F32)]
        + lines
        + [pltpu.VMEM((16, 128), F32), pltpu.VMEM((512, 2048), BF16), pltpu.VMEM((128, 2048), BF16)]
        + [pltpu.SemaphoreType.DMA((5,))],
        compiler_params=vmem_params(16),
        cost_estimate=light,
    )(*(pltpu.with_memory_space_constraint(x, pltpu.HBM) for x in records))
    got = lax.all_to_all(send, "blocks", split_axis=0, concat_axis=0, tiled=True)

    prior, inv_volume, off, coord, vol_cot = (
        pltpu.with_memory_space_constraint(x, pltpu.HBM) for x in (prior, inv_volume, off, coord, vol_cot)
    )
    three, one = pltpu.VMEM((48, NJ, NK), F32), pltpu.VMEM((16, NJ, NK), F32)
    up1, dn1 = pl.pallas_call(
        pack_warp_kernel,
        name="pack_warp",
        in_specs=[hbm] * 2,
        out_specs=whole(2),
        out_shape=(shape(65, 8, 256), shape(65, 8, 256)),
        scratch_shapes=[three, one, pltpu.SemaphoreType.DMA((4,))],
        compiler_params=vmem_params(5),
        cost_estimate=light,
    )(*(pltpu.with_memory_space_constraint(x, pltpu.HBM) for x in lax.optimization_barrier((prior, inv_volume, send))[:2]))
    tied = lax.optimization_barrier((up1, prior, inv_volume, off, coord, vol_cot))[1:]
    prior_t, inv_t, off_t, coord_t, vol_t = (pltpu.with_memory_space_constraint(x, pltpu.HBM) for x in tied)
    up1 = shifted(up1, "blocks", 1)
    dn1 = shifted(dn1, "blocks", -1)
    rt, lf, up2, dn2 = pl.pallas_call(
        pack_rest_kernel,
        name="pack_rest",
        in_specs=[hbm] * 5,
        out_specs=whole(4),
        out_shape=(shape(22, 32, 128), shape(22, 32, 128), shape(87, 8, 256), shape(87, 8, 256)),
        scratch_shapes=[three, one, three, three, one, pltpu.SemaphoreType.DMA((11,))],
        compiler_params=vmem_params(12),
        cost_estimate=light,
    )(prior_t, inv_t, off_t, coord_t, vol_t)
    from_lf = shifted(rt, "span", 1)
    from_rt = shifted(lf, "span", -1)
    surf, srt, slf = pl.pallas_call(
        surface_kernel,
        name="surface",
        in_specs=whole(1),
        out_specs=whole(3),
        out_shape=(shape(3, 64, 256), shape(3, 64, 128), shape(3, 64, 128)),
        scratch_shapes=[
            pltpu.VMEM((288, 4096), BF16),
            pltpu.VMEM((256, 4096), BF16),
            pltpu.VMEM((144, 4096), BF16),
            pltpu.VMEM((256, 4096), BF16),
            pltpu.VMEM((144, 4096), BF16),
            pltpu.VMEM((256, 4096), BF16),
        ],
        compiler_params=vmem_params(16),
        cost_estimate=light,
    )(got)
    surf_lf = shifted(srt, "span", 1)
    surf_rt = shifted(slf, "span", -1)

    cup, cdn = pl.pallas_call(
        corner_kernel,
        name="corner",
        in_specs=whole(2),
        out_specs=whole(2),
        out_shape=(shape(56, 8, 128), shape(56, 8, 128)),
        compiler_params=vmem_params(4),
        cost_estimate=light,
    )(*lax.optimization_barrier((from_lf, from_rt, surf))[:2])
    cup = shifted(cup, "blocks", 1)
    cdn = shifted(cdn, "blocks", -1)
    up2, dn2, up1, dn1, cup, cdn, surf_lf, surf_rt = lax.optimization_barrier(
        (up2, dn2, up1, dn1, cup, cdn, surf_lf, surf_rt)
    )
    up2 = shifted(up2, "blocks", 1)
    dn2 = shifted(dn2, "blocks", -1)

    big = pltpu.VMEM((48, 3, ROWS, 128), F32)
    warp_field, field, relax = pl.pallas_call(
        warp_kernel,
        name="warp",
        in_specs=[hbm] * 2 + whole(9),
        out_specs=[hbm] + whole(2),
        out_shape=(shape(48, NJ, NK), shape(48, 3, ROWS, 128), shape(16, 3, ROWS, 128)),
        scratch_shapes=[big, pltpu.SemaphoreType.DMA((20,))],
        compiler_params=vmem_params(16),
        cost_estimate=pl.CostEstimate(flops=60_000_000, bytes_accessed=20_000_000, transcendentals=0),
    )(prior, inv_volume, surf, surf_lf, surf_rt, up1, dn1, from_lf, from_rt, cup, cdn)
    adjoint, reply = pl.pallas_call(
        adjoint_kernel,
        name="adjoint",
        in_specs=[hbm] * 3 + whole(9),
        out_specs=[hbm] + whole(1),
        out_shape=(shape(48, NJ, NK), shape(32, 3, 128)),
        scratch_shapes=[big] * 4
        + [pltpu.VMEM((16, 3, ROWS, 128), F32)]
        + [pltpu.VMEM((3, 3, ROWS, 128), F32)] * 2
        + [pltpu.SemaphoreType.DMA((18,))],
        compiler_params=vmem_params(25),
        cost_estimate=pl.CostEstimate(flops=60_000_000, bytes_accessed=20_000_000, transcendentals=0),
    )(off, coord, vol_cot, field, relax, up2, dn2, from_lf, from_rt, cup, cdn, got)
    back = lax.all_to_all(reply, "blocks", split_axis=0, concat_axis=0, tiled=True)
    struct_sens = pl.pallas_call(
        sens_kernel,
        name="sens",
        in_specs=whole(2),
        out_specs=whole(1)[0],
        out_shape=shape(3, 512),
        scratch_shapes=[pltpu.VMEM((48, 4096), BF16), pltpu.VMEM((128, 4096), BF16)],
        compiler_params=vmem_params(16),
    )(back, slots)
    return (
        warp_field.reshape(3, NI, NJ, NK),
        adjoint.reshape(3, NI, NJ, NK),
        struct_sens,
    )


def solution(mesh):
    placed = (
        P(None, ("blocks", "span")),
        P(("blocks", "span")),
        P(("blocks", "span"), None),
        P(("blocks", "span")),
        P(("blocks", "span")),
        P(None, None, "blocks", "span"),
        P(None, None, "blocks", "span"),
        P(None, "blocks", "span"),
        P(None, None, "blocks", "span"),
        P(None, "blocks", "span"),
    )
    return jax.shard_map(
        body,
        mesh=mesh,
        in_specs=placed,
        out_specs=(
            P(None, None, "blocks", "span"),
            P(None, None, "blocks", "span"),
            P(None, ("blocks", "span")),
        ),
        check_vma=False,
    )
```

```python
import jax
import jax.numpy as jnp
from jax import lax
from jax.experimental import pallas as pl
from jax.experimental.pallas import tpu as pltpu
from jax.sharding import PartitionSpec as P

SWEEPS = 4
CAPACITY = 128
F32 = jnp.float32
BF16 = jnp.bfloat16
NT = (((1,), (1,)), ((), ()))

NI, NJ, NK = 16, 32, 256
ROWS, LANES = 64, 384
TOP = 16
TILES = tuple(range(1, 7))


def vmem_params(mib):
    return pltpu.CompilerParams(vmem_limit_bytes=mib << 20)


def whole(n):
    return [pl.BlockSpec(memory_space=pltpu.VMEM)] * n


def halves(x):
    hi = x.astype(BF16)
    rest = x - hi.astype(F32)
    mid = rest.astype(BF16)
    lo = (rest - mid.astype(F32)).astype(BF16)
    return hi, mid, lo


def hot(count, row):
    return (lax.broadcasted_iota(jnp.int32, (count, CAPACITY), 0) == row).astype(F32).astype(BF16)


def ends():
    block, slab = lax.axis_index("blocks"), lax.axis_index("span")
    last_block = block == lax.axis_size("blocks") - 1
    last_slab = slab == lax.axis_size("span") - 1
    return block == 0, last_block, slab == 0, last_slab


def unless(flag):
    return jnp.where(flag, 0.0, 1.0).astype(F32)


def rolled(x, by):
    by = by % x.shape[-1]
    return pltpu.roll(x, by, x.ndim - 1) if by else x


def pack_sides(field, base, rt, lf, keep_rt, keep_lf):
    slot = lax.broadcasted_iota(jnp.int32, (NJ, 128), 1) // 16
    groups = field.shape[0] // 8

    def one(g, carry):
        right = jnp.zeros((NJ, 128), F32)
        left = jnp.zeros((NJ, 128), F32)
        for q in range(8):
            plane = g * 8 + q
            right = jnp.where(slot == q, rolled(field[plane, :, 128:256], 16 * q + 16), right)
            left = jnp.where(slot == q, rolled(field[plane, :, 0:128], 16 * q), left)
        rt[base + g] = right * keep_rt
        lf[base + g] = left * keep_lf
        return carry

    lax.fori_loop(0, groups, one, 0)
    return base + groups


def load(sems, *pairs):
    copies = [pltpu.make_async_copy(src, dst, sems.at[n]) for n, (src, dst) in enumerate(pairs)]
    for c in copies:
        c.start()
    for c in copies:
        c.wait()


def pack_warp_kernel(prior_hbm, inv_hbm, up, dn, prior, inv, sems):
    first_block, last_block, _, _ = ends()
    load(sems, *[(prior_hbm.at[16 * v : 16 * v + 16], prior.at[16 * v : 16 * v + 16]) for v in range(3)], (inv_hbm, inv))
    keep_up, keep_dn = unless(last_block), unless(first_block)
    for v in range(3):
        up[15 * v : 15 * v + 15] = prior[16 * v + 1 : 16 * v + 16, 24:32, :] * keep_up
        dn[15 * v : 15 * v + 15] = prior[16 * v + 1 : 16 * v + 16, 0:8, :] * keep_dn
    up[45:59] = inv[1:15, 24:32, :] * keep_up
    dn[45:59] = inv[1:15, 0:8, :] * keep_dn
    for n in range(45):
        p = 16 * (n // 15) + n % 15 + 1
        up[59 + n // 8, n % 8 : n % 8 + 1, :] = prior[p, 23:24, :] * keep_up
        dn[59 + n // 8, n % 8 : n % 8 + 1, :] = prior[p, 8:9, :] * keep_dn


def pack_rest_kernel(prior_hbm, inv_hbm, off_hbm, coord_hbm, vol_hbm, rt, lf, up, dn, prior, inv, offset, coord, vol, sems):
    first_block, last_block, first_slab, last_slab = ends()
    keep_up, keep_dn = unless(last_block), unless(first_block)
    pairs = [(inv_hbm, inv), (vol_hbm, vol)]
    for v in range(3):
        at = slice(16 * v, 16 * v + 16)
        pairs += [(prior_hbm.at[at], prior.at[at]), (off_hbm.at[at], offset.at[at]), (coord_hbm.at[at], coord.at[at])]
    copies = [pltpu.make_async_copy(src, dst, sems.at[n]) for n, (src, dst) in enumerate(pairs)]
    for c in copies:
        c.start()
    base = 0
    for field, waits in ((prior, (2, 5, 8)), (inv, (0,)), (offset, (3, 6, 9)), (coord, (4, 7, 10)), (vol, (1,))):
        for n in waits:
            copies[n].wait()
        base = pack_sides(field, base, rt, lf, unless(last_slab), unless(first_slab))
    start = 30
    for p in range(48):
        line = slice(p % 8, p % 8 + 1)
        for j in range(5):
            up[5 * (p // 8) + j, line, :] = offset[p, 27 + j : 28 + j, :]
            dn[5 * (p // 8) + j, line, :] = offset[p, j : j + 1, :]
    up[start : start + 15] = vol[0:15, 24:32, :] * keep_up
    dn[start : start + 15] = vol[0:15, 0:8, :] * keep_dn
    start += 15
    low = lax.broadcasted_iota(jnp.int32, (8, NK), 0) < 4
    for m in range(24):
        other = pltpu.roll(coord[m + 24, 24:32, :], 4, 0)
        up[start + m] = jnp.where(low, other, coord[m, 24:32, :]) * keep_up
        other = pltpu.roll(coord[m + 24, 0:8, :], 4, 0)
        dn[start + m] = jnp.where(low, coord[m, 0:8, :], other) * keep_dn


def corner_kernel(from_lf, from_rt, up, dn):
    first_block, last_block, _, _ = ends()
    keep_up, keep_dn = unless(last_block), unless(first_block)
    for s, side in enumerate((from_lf, from_rt)):
        b = 28 * s
        up[b : b + 22] = side[:, 24:32, :] * keep_up
        dn[b : b + 22] = side[:, 0:8, :] * keep_dn
        up[b + 22 : b + 28] = side[0:6, 16:24, :] * keep_up
        dn[b + 22 : b + 28] = side[0:6, 8:16, :] * keep_dn


def route_kernel(
    disp_hbm, blk_hbm, node_hbm, struct_hbm, weight_hbm, send, slots,
    disp, blk, node, struct, weight, table, lhs, rhs, sems,
):
    load(sems, (blk_hbm, blk), (struct_hbm, struct), (disp_hbm, disp), (weight_hbm, weight), (node_hbm, node))
    first = lax.broadcasted_iota(jnp.int32, (32, 128), 0)
    table[...] = jnp.zeros((16, 128), F32)
    for a in range(4):
        table[4 * a : 4 * a + 3, :] = disp[:, 128 * a : 128 * a + 128]
    parts = jnp.concatenate(halves(table[...]), axis=0)
    earlier = (
        lax.broadcasted_iota(jnp.int32, (128, 128), 0) < lax.broadcasted_iota(jnp.int32, (128, 128), 1)
    ).astype(F32).astype(BF16)
    ones = jnp.ones((128, 128), BF16)
    named = [first == blk[c : c + 1, :] for c in range(16)]
    named = [x.astype(F32) for x in named]
    stacked = jnp.concatenate([x.astype(BF16) for x in named], axis=0)
    before = jnp.dot(stacked, earlier, preferred_element_type=F32)
    totals = jnp.dot(stacked, ones, preferred_element_type=F32)
    running = jnp.zeros((32, 128), F32)
    quarter = lax.broadcasted_iota(jnp.int32, (16, 128), 0) // 4
    for c in range(16):
        at = slice(128 * c, 128 * c + 128)
        rank = jnp.sum(named[c] * (before[32 * c : 32 * c + 32] + running), axis=0, keepdims=True)
        running = running + totals[32 * c : 32 * c + 32]
        rhs[:, at] = hot(128, rank.astype(jnp.int32))
        s = struct[c : c + 1, :]
        high, low = s // 128, s % 128
        got = jnp.dot(parts, hot(128, low), preferred_element_type=F32)
        got = got[0:16] + got[16:32] + got[32:48]
        got = jnp.where(quarter == high, got, 0.0)
        got = got[0:8] + got[8:16]
        got = got[0:4] + got[4:8]
        w = weight[c : c + 1, :]
        moved = halves(got[0:3] * w)
        wparts = halves(w)
        n = node[c : c + 1, :]
        rows = [part[v : v + 1] for v in range(3) for part in moved]
        rows += [(n // 256).astype(F32).astype(BF16), (n % 256).astype(F32).astype(BF16)]
        rows += list(wparts)
        rows += [high.astype(F32).astype(BF16), low.astype(F32).astype(BF16)]
        mine = named[c].astype(BF16)
        for p, row in enumerate(rows):
            lhs[32 * p : 32 * p + 32, at] = mine * row
    out = lax.dot_general(lhs[...], rhs[...], NT, preferred_element_type=F32)
    row = lambda p: out[32 * p : 32 * p + 32]
    payload = [row(3 * v) + row(3 * v + 1) + row(3 * v + 2) for v in range(3)]
    payload.append(row(9) * 256.0 + row(10))
    slots[0] = row(11) + row(12) + row(13)
    slots[1] = row(14) * 128.0 + row(15)
    for p, x in enumerate(payload):
        for g in range(32):
            line = x[g : g + 1]
            send[g, 4 + p : 5 + p, :] = line
            if g < 31:
                send[g + 1, p : p + 1, :] = line
            if g > 0:
                send[g - 1, 8 + p : 9 + p, :] = line
    send[0, 0:4, :] = jnp.zeros((4, 128), F32)
    send[31, 8:12, :] = jnp.zeros((4, 128), F32)


def surface_kernel(got, surf, rt, lf, lhs, rhs, lhs_lo, rhs_lo, lhs_up, rhs_up):
    _, _, first_slab, last_slab = ends()
    for s in range(32):
        at = slice(128 * s, 128 * s + 128)
        for kind, (left, right, count, shift) in enumerate(
            ((lhs_lo, rhs_lo, 16, 16), (lhs, rhs, 32, 0), (lhs_up, rhs_up, 16, 0))
        ):
            n = got[s, 4 * kind + 3 : 4 * kind + 4, :].astype(jnp.int32)
            right[:, at] = hot(256, n % 256)
            rows = hot(count, n // 256 - shift)
            parts = halves(got[s, 4 * kind : 4 * kind + 3, :])
            for v in range(3):
                for h in range(3):
                    line = (3 * v + h) * count
                    left[line : line + count, at] = rows * parts[h][v : v + 1]
    for left, right, count, base in ((lhs_lo, rhs_lo, 16, 0), (lhs, rhs, 32, 16), (lhs_up, rhs_up, 16, 48)):
        out = lax.dot_general(left[...], right[...], NT, preferred_element_type=F32)
        for v in range(3):
            b = 3 * v * count
            surf[v, base : base + count, :] = (
                out[b : b + count] + out[b + count : b + 2 * count] + out[b + 2 * count : b + 3 * count]
            )
    rt[...] = surf[:, :, 128:256] * unless(last_slab)
    lf[...] = surf[:, :, 0:128] * unless(first_slab)


def copier(sems):
    copies = []

    def copy(src, dst):
        c = pltpu.make_async_copy(src, dst, sems.at[len(copies)])
        c.start()
        copies.append(c)

    return copies, copy


def bring(copy, field, ext):
    for lt in range(2):
        copy(field.at[:, :, 128 * lt : 128 * lt + 128], ext.at[:, lt, TOP : TOP + NJ, :])


def bring_rims(copy, up, dn, start, ext, first, count):
    for lt in range(2):
        at = slice(128 * lt, 128 * lt + 128)
        copy(up.at[start : start + count, :, at], ext.at[first : first + count, lt, 8:16, :])
        copy(dn.at[start : start + count, :, at], ext.at[first : first + count, lt, 48:56, :])


def bring_sides(exts, base, lf, rt, cup, cdn):
    side = lax.broadcasted_iota(jnp.int32, (8, 128), 1) < 64
    for ext, deep in exts:
        groups = ext.shape[0] // 8

        def one(g, carry, ext=ext, base=base, deep=deep):
            for q in range(8):
                p = g * 8 + q

                def tile(from_rt, from_lf):
                    return jnp.where(side, rolled(from_rt, -16 * q), rolled(from_lf, 112 - 16 * q))

                for t in range(4):
                    rows = slice(8 * t, 8 * t + 8)
                    ext[p, 2, TOP + 8 * t : TOP + 8 * t + 8, :] = tile(rt[base + g, rows, :], lf[base + g, rows, :])
                ext[p, 2, 8:16, :] = tile(cup[28 + base + g], cup[base + g])
                ext[p, 2, 48:56, :] = tile(cdn[28 + base + g], cdn[base + g])
                if deep:
                    ext[p, 2, 0:8, :] = tile(cup[50 + g], cup[22 + g])
                    ext[p, 2, 56:64, :] = tile(cdn[50 + g], cdn[22 + g])
            return carry

        lax.fori_loop(0, groups, one, 0)
        base += groups


def beside(tiles, masks):
    first, last = masks
    out = []
    for n, c in enumerate(tiles):
        before = pltpu.roll(jnp.where(last, tiles[(n + 2) % 3], c), 1, 1)
        after = pltpu.roll(jnp.where(first, tiles[(n + 1) % 3], c), 127, 1)
        out.append(before + after)
    return out


def lane_masks():
    lane = lax.broadcasted_iota(jnp.int32, (8, 128), 1)
    return lane == 0, lane == 127


def warp_kernel(prior, inv, surf, surf_lf, surf_rt, up, dn, lf, rt, cup, cdn, warp_out, w0, relax, w1, sems):
    copies, copy = copier(sems)
    bring(copy, prior, w0)
    bring(copy, inv, relax)
    for v in range(3):
        bring_rims(copy, up, dn, 15 * v, w0, 16 * v + 1, 15)
    bring_rims(copy, up, dn, 45, relax, 1, 14)
    bring_sides(((w0, True), (relax, False)), 0, lf, rt, cup, cdn)
    for n in range(45):
        p = 16 * (n // 15) + n % 15 + 1
        for lt in range(2):
            at = slice(128 * lt, 128 * lt + 128)
            w0[p, lt, 7:8, :] = up[59 + n // 8, n % 8 : n % 8 + 1, at]
            w0[p, lt, 56:57, :] = dn[59 + n // 8, n % 8 : n % 8 + 1, at]
    for c in copies:
        c.wait()
    wide = lax.broadcasted_iota(jnp.int32, (ROWS, 128), 1) < 64
    for v in range(3):
        for lt in range(2):
            w0[16 * v, lt] = surf[v, :, 128 * lt : 128 * lt + 128]
        w0[16 * v, 2] = jnp.where(wide, surf_rt[v], surf_lf[v])
    masks = lane_masks()

    def sweep(src, dst):
        def component(v, carry):
            b = 16 * v
            for t in TILES:
                r, below, above = (slice(8 * t + d, 8 * t + 8 + d) for d in (0, 1, -1))
                prev = [src[b, n, r, :] for n in range(3)]
                cur = [src[b + 1, n, r, :] for n in range(3)]
                for n in range(3):
                    dst[b, n, r, :] = prev[n]
                for i in range(1, NI - 1):
                    p = b + i
                    nxt = [src[p + 1, n, r, :] for n in range(3)]
                    flat = beside(cur, masks)
                    for n in range(3):
                        total = ((src[p, n, below, :] + src[p, n, above, :]) + flat[n]) + (nxt[n] + prev[n])
                        dst[p, n, r, :] = cur[n] + relax[i, n, r, :] * (total - 6.0 * cur[n])
                    prev, cur = cur, nxt
                for n in range(3):
                    dst[b + NI - 1, n, r, :] = cur[n]
            return carry

        lax.fori_loop(0, 3, component, 0)

    sweep(w0, w1)
    sweep(w1, w0)
    sweep(w0, w1)
    sweep(w1, w0)
    copies, copy = copier(sems)
    for lt in range(2):
        copy(w0.at[:, lt, TOP : TOP + NJ, :], warp_out.at[:, :, 128 * lt : 128 * lt + 128])
    for c in copies:
        c.wait()


def cross(x, y, w):
    return (
        w * (x[1] * y[2] - x[2] * y[1]),
        w * (x[2] * y[0] - x[0] * y[2]),
        w * (x[0] * y[1] - x[1] * y[0]),
    )


def adjoint_kernel(
    offset, coord, vol, field, relax, up, dn, lf, rt, cup, cdn, got,
    adj_out, reply,
    s, a, f0, f1, cell, gi, gj, sems,
):
    copies, copy = copier(sems)
    bring(copy, offset, s)
    bring(copy, coord, a)
    bring(copy, vol, cell)
    bring_rims(copy, up, dn, 30, cell, 0, 15)
    bring_rims(copy, up, dn, 45, a, 0, 24)
    for p in range(48):
        line = slice(p % 8, p % 8 + 1)
        for lt in range(2):
            at = slice(128 * lt, 128 * lt + 128)
            s[p, lt, 8:11, :] = jnp.zeros((3, 128), F32)
            s[p, lt, 53:56, :] = jnp.zeros((3, 128), F32)
            for j in range(5):
                s[p, lt, 11 + j : 12 + j, :] = up[5 * (p // 8) + j, line, at]
                s[p, lt, 48 + j : 49 + j, :] = dn[5 * (p // 8) + j, line, at]
    bring_sides(((s, False), (a, False), (cell, False)), 8, lf, rt, cup, cdn)
    for m in range(24):
        for lt in range(2):
            at = slice(128 * lt, 128 * lt + 128)
            a[m + 24, lt, 8:16, :] = pltpu.roll(up[45 + m, :, at], 4, 0)
            a[m + 24, lt, 48:56, :] = pltpu.roll(dn[45 + m, :, at], 4, 0)
    for c in copies:
        c.wait()
    _, last_block, _, last_slab = ends()

    @pl.when(last_block)
    def _():
        for i in range(NI):
            for n in range(3):
                cell[i, n, TOP + NJ - 1 : TOP + NJ, :] = jnp.zeros((1, 128), F32)

    @pl.when(last_slab)
    def _():
        lane = lax.broadcasted_iota(jnp.int32, (48, 128), 1)
        for i in range(NI):
            cell[i, 1, 8:56, :] = jnp.where(lane == 127, 0.0, cell[i, 1, 8:56, :])

    def shape_plane(p, carry):
        s[p, :, 8:56, :] = s[p, :, 8:56, :] + field[p, :, 8:56, :]
        return carry

    lax.fori_loop(0, 48, shape_plane, 0)
    gi[...] = jnp.zeros((3, 3, ROWS, 128), F32)
    gj[:, :, 0:8, :] = jnp.zeros((3, 3, 8, 128), F32)
    first, last = masks = lane_masks()

    def grad_plane(i, carry):
        for t in TILES:
            r, below, above = (slice(8 * t + d, 8 * t + 8 + d) for d in (0, 1, -1))
            here = [[s[16 * v + i, n, r, :] for n in range(3)] for v in range(3)]
            along, held = [], []
            for n in range(3):
                ei = [s[16 * v + i + 1, n, r, :] - here[v][n] for v in range(3)]
                ej = [s[16 * v + i, n, below, :] - here[v][n] for v in range(3)]
                ek = [
                    pltpu.roll(jnp.where(first, here[v][(n + 1) % 3], here[v][n]), 127, 1) - here[v][n]
                    for v in range(3)
                ]
                ei[0], ej[1], ek[2] = ei[0] + 1.0, ej[1] + 1.0, ek[2] + 1.0
                w = cell[i, n, r, :]
                new_i, new_j, new_k = cross(ej, ek, w), cross(ek, ei, w), cross(ei, ej, w)
                along.append(new_k)
                held.append([])
                for v in range(3):
                    p = 16 * v + i
                    gj[v, n, r, :] = new_j[v]
                    value = a[p, n, r, :] - new_i[v] + gi[v, n, r, :] - new_j[v]
                    held[n].append(value + gj[v, n, above, :] - new_k[v])
                    gi[v, n, r, :] = new_i[v]
            for n in range(3):
                rel = jnp.where(i > 0, relax[i, n, r, :], 0.0)
                for v in range(3):
                    p = 16 * v + i
                    value = held[n][v] + pltpu.roll(jnp.where(last, along[(n + 2) % 3][v], along[n][v]), 1, 1)
                    a[p, n, r, :] = value
                    f0[p, n, r, :] = rel * value
        return carry

    lax.fori_loop(0, NI - 1, grad_plane, 0)
    for v in range(3):
        p = 16 * v + NI - 1
        a[p, :, 8:56, :] = a[p, :, 8:56, :] + gi[v, :, 8:56, :]

    def sweep(src, dst, final):
        lanes = range(2) if final else range(3)

        def component(v, carry):
            b = 16 * v
            for t in TILES[1:-1] if final else TILES:
                r, below, above = (slice(8 * t + d, 8 * t + 8 + d) for d in (0, 1, -1))
                prev = None
                cur = [src[b + 1, n, r, :] for n in range(3)]
                for n in lanes:
                    a[b, n, r, :] = a[b, n, r, :] + cur[n]
                for i in range(1, NI - 1):
                    p = b + i
                    nxt = [src[p + 1, n, r, :] for n in range(3)] if i < NI - 2 else None
                    flat = beside(cur, masks)
                    for n in lanes:
                        if prev is None:
                            sides = nxt[n]
                        elif nxt is None:
                            sides = prev[n]
                        else:
                            sides = nxt[n] + prev[n]
                        total = ((src[p, n, below, :] + src[p, n, above, :]) + flat[n]) + sides
                        new = a[p, n, r, :] + (total - 6.0 * cur[n])
                        a[p, n, r, :] = new
                        if not final:
                            dst[p, n, r, :] = relax[i, n, r, :] * new
                    prev, cur = cur, nxt
                for n in lanes:
                    a[b + NI - 1, n, r, :] = a[b + NI - 1, n, r, :] + prev[n]
            return carry

        lax.fori_loop(0, 3, component, 0)

    sweep(f0, f1, False)
    sweep(f1, f0, False)
    sweep(f0, f1, False)
    sweep(f1, f0, True)
    copies, copy = copier(sems)
    for lt in range(2):
        copy(a.at[:, lt, TOP : TOP + NJ, :], adj_out.at[:, :, 128 * lt : 128 * lt + 128])

    wall = [jnp.concatenate([a[16 * v, lt, TOP : TOP + NJ, :] for lt in range(2)], axis=1) for v in range(3)]
    table = jnp.concatenate([h for v in range(3) for h in halves(wall[v])], axis=0)
    lines = lax.broadcasted_iota(jnp.int32, (32, 128), 0)
    for q in range(32):
        n = got[q, 7:8, :].astype(jnp.int32)
        picked = jnp.dot(table, hot(256, n % 256), preferred_element_type=F32)
        mine = lines == n // 256
        for v in range(3):
            b = 96 * v
            x = picked[b : b + 32] + picked[b + 32 : b + 64] + picked[b + 64 : b + 96]
            reply[q, v : v + 1, :] = jnp.sum(jnp.where(mine, x, 0.0), axis=0, keepdims=True)
    for c in copies:
        c.wait()


def sens_kernel(back, slots, out, lhs, rhs):
    quarter = lax.broadcasted_iota(jnp.int32, (4, 128), 0)
    for g in range(32):
        at = slice(128 * g, 128 * g + 128)
        n = slots[1, g : g + 1, :].astype(jnp.int32)
        high, low = n // 128, n % 128
        rhs[:, at] = hot(128, low)
        value = back[g] * slots[0, g : g + 1, :]
        rows = jnp.concatenate([jnp.where(quarter == high, value[v : v + 1], 0.0) for v in range(3)] + [jnp.zeros((4, 128), F32)], axis=0)
        lhs[:, at] = jnp.concatenate(halves(rows), axis=0)
    total = lax.dot_general(lhs[...], rhs[...], NT, preferred_element_type=F32)
    total = total[0:16] + total[16:32] + total[32:48]
    for v in range(3):
        for q in range(4):
            out[v : v + 1, 128 * q : 128 * q + 128] = total[4 * v + q : 4 * v + q + 1]


def shifted(x, axis, by):
    size = lax.axis_size(axis)
    return lax.ppermute(x, axis, [(i, (i + by) % size) for i in range(size)])


def shape(*dims):
    return jax.ShapeDtypeStruct(dims, F32)


def body(struct_disp, rec_struct, rec_block, rec_node, rec_weight, offset, prior_warp, inv_volume, coord_cot, vol_cot):
    prior = prior_warp.reshape(48, NJ, NK)
    off = offset.reshape(48, NJ, NK)
    coord = coord_cot.reshape(48, NJ, NK)

    hbm = pl.BlockSpec(memory_space=pltpu.HBM)
    light = pl.CostEstimate(flops=1000, bytes_accessed=1000, transcendentals=0)
    records = (struct_disp, *(x.reshape(16, 128) for x in (rec_block, rec_node, rec_struct, rec_weight)))
    lines = [pltpu.VMEM((16, 128), dtype) for dtype in (jnp.int32, jnp.int32, jnp.int32, F32)]
    send, slots = pl.pallas_call(
        route_kernel,
        name="route",
        in_specs=[hbm] * 5,
        out_specs=whole(2),
        out_shape=(shape(32, 12, 128), shape(2, 32, 128)),
        scratch_shapes=[pltpu.VMEM((3, 512), F32)]
        + lines
        + [pltpu.VMEM((16, 128), F32), pltpu.VMEM((512, 2048), BF16), pltpu.VMEM((128, 2048), BF16)]
        + [pltpu.SemaphoreType.DMA((5,))],
        compiler_params=vmem_params(16),
        cost_estimate=light,
    )(*(pltpu.with_memory_space_constraint(x, pltpu.HBM) for x in records))
    got = lax.all_to_all(send, "blocks", split_axis=0, concat_axis=0, tiled=True)

    prior, inv_volume, off, coord, vol_cot = (
        pltpu.with_memory_space_constraint(x, pltpu.HBM) for x in (prior, inv_volume, off, coord, vol_cot)
    )
    three, one = pltpu.VMEM((48, NJ, NK), F32), pltpu.VMEM((16, NJ, NK), F32)
    up1, dn1 = pl.pallas_call(
        pack_warp_kernel,
        name="pack_warp",
        in_specs=[hbm] * 2,
        out_specs=whole(2),
        out_shape=(shape(65, 8, 256), shape(65, 8, 256)),
        scratch_shapes=[three, one, pltpu.SemaphoreType.DMA((4,))],
        compiler_params=vmem_params(5),
        cost_estimate=light,
    )(*(pltpu.with_memory_space_constraint(x, pltpu.HBM) for x in lax.optimization_barrier((prior, inv_volume, send))[:2]))
    tied = lax.optimization_barrier((up1, prior, inv_volume, off, coord, vol_cot))[1:]
    prior_t, inv_t, off_t, coord_t, vol_t = (pltpu.with_memory_space_constraint(x, pltpu.HBM) for x in tied)
    up1 = shifted(up1, "blocks", 1)
    dn1 = shifted(dn1, "blocks", -1)
    rt, lf, up2, dn2 = pl.pallas_call(
        pack_rest_kernel,
        name="pack_rest",
        in_specs=[hbm] * 5,
        out_specs=whole(4),
        out_shape=(shape(22, 32, 128), shape(22, 32, 128), shape(69, 8, 256), shape(69, 8, 256)),
        scratch_shapes=[three, one, three, three, one, pltpu.SemaphoreType.DMA((11,))],
        compiler_params=vmem_params(12),
        cost_estimate=light,
    )(prior_t, inv_t, off_t, coord_t, vol_t)
    from_lf = shifted(rt, "span", 1)
    from_rt = shifted(lf, "span", -1)
    surf, srt, slf = pl.pallas_call(
        surface_kernel,
        name="surface",
        in_specs=whole(1),
        out_specs=whole(3),
        out_shape=(shape(3, 64, 256), shape(3, 64, 128), shape(3, 64, 128)),
        scratch_shapes=[
            pltpu.VMEM((288, 4096), BF16),
            pltpu.VMEM((256, 4096), BF16),
            pltpu.VMEM((144, 4096), BF16),
            pltpu.VMEM((256, 4096), BF16),
            pltpu.VMEM((144, 4096), BF16),
            pltpu.VMEM((256, 4096), BF16),
        ],
        compiler_params=vmem_params(16),
        cost_estimate=light,
    )(got)
    surf_lf = shifted(srt, "span", 1)
    surf_rt = shifted(slf, "span", -1)

    cup, cdn = pl.pallas_call(
        corner_kernel,
        name="corner",
        in_specs=whole(2),
        out_specs=whole(2),
        out_shape=(shape(56, 8, 128), shape(56, 8, 128)),
        compiler_params=vmem_params(4),
        cost_estimate=light,
    )(*lax.optimization_barrier((from_lf, from_rt, surf))[:2])
    cup = shifted(cup, "blocks", 1)
    cdn = shifted(cdn, "blocks", -1)
    up2, dn2, up1, dn1, cup, cdn, surf_lf, surf_rt = lax.optimization_barrier(
        (up2, dn2, up1, dn1, cup, cdn, surf_lf, surf_rt)
    )
    up2 = shifted(up2, "blocks", 1)
    dn2 = shifted(dn2, "blocks", -1)

    big = pltpu.VMEM((48, 3, ROWS, 128), F32)
    warp_field, field, relax = pl.pallas_call(
        warp_kernel,
        name="warp",
        in_specs=[hbm] * 2 + whole(9),
        out_specs=[hbm] + whole(2),
        out_shape=(shape(48, NJ, NK), shape(48, 3, ROWS, 128), shape(16, 3, ROWS, 128)),
        scratch_shapes=[big, pltpu.SemaphoreType.DMA((20,))],
        compiler_params=vmem_params(16),
        cost_estimate=pl.CostEstimate(flops=60_000_000, bytes_accessed=20_000_000, transcendentals=0),
    )(prior, inv_volume, surf, surf_lf, surf_rt, up1, dn1, from_lf, from_rt, cup, cdn)
    adjoint, reply = pl.pallas_call(
        adjoint_kernel,
        name="adjoint",
        in_specs=[hbm] * 3 + whole(9),
        out_specs=[hbm] + whole(1),
        out_shape=(shape(48, NJ, NK), shape(32, 3, 128)),
        scratch_shapes=[big] * 4
        + [pltpu.VMEM((16, 3, ROWS, 128), F32)]
        + [pltpu.VMEM((3, 3, ROWS, 128), F32)] * 2
        + [pltpu.SemaphoreType.DMA((18,))],
        compiler_params=vmem_params(25),
        cost_estimate=pl.CostEstimate(flops=60_000_000, bytes_accessed=20_000_000, transcendentals=0),
    )(off, coord, vol_cot, field, relax, up2, dn2, from_lf, from_rt, cup, cdn, got)
    back = lax.all_to_all(reply, "blocks", split_axis=0, concat_axis=0, tiled=True)
    struct_sens = pl.pallas_call(
        sens_kernel,
        name="sens",
        in_specs=whole(2),
        out_specs=whole(1)[0],
        out_shape=shape(3, 512),
        scratch_shapes=[pltpu.VMEM((48, 4096), BF16), pltpu.VMEM((128, 4096), BF16)],
        compiler_params=vmem_params(16),
    )(back, slots)
    return (
        warp_field.reshape(3, NI, NJ, NK),
        adjoint.reshape(3, NI, NJ, NK),
        struct_sens,
    )


def solution(mesh):
    placed = (
        P(None, ("blocks", "span")),
        P(("blocks", "span")),
        P(("blocks", "span"), None),
        P(("blocks", "span")),
        P(("blocks", "span")),
        P(None, None, "blocks", "span"),
        P(None, None, "blocks", "span"),
        P(None, "blocks", "span"),
        P(None, None, "blocks", "span"),
        P(None, "blocks", "span"),
    )
    return jax.shard_map(
        body,
        mesh=mesh,
        in_specs=placed,
        out_specs=(
            P(None, None, "blocks", "span"),
            P(None, None, "blocks", "span"),
            P(None, ("blocks", "span")),
        ),
        check_vma=False,
    )
```

```python
import jax
import jax.numpy as jnp
from jax import lax
from jax.experimental import pallas as pl
from jax.experimental.pallas import tpu as pltpu
from jax.sharding import PartitionSpec as P

SWEEPS = 4
CAPACITY = 128
F32 = jnp.float32
BF16 = jnp.bfloat16
NT = (((1,), (1,)), ((), ()))

NI, NJ, NK = 16, 32, 256
ROWS, LANES = 64, 384
TOP = 16
TILES = tuple(range(1, 7))


def vmem_params(mib):
    return pltpu.CompilerParams(vmem_limit_bytes=mib << 20)


def whole(n):
    return [pl.BlockSpec(memory_space=pltpu.VMEM)] * n


def halves(x):
    hi = x.astype(BF16)
    rest = x - hi.astype(F32)
    mid = rest.astype(BF16)
    lo = (rest - mid.astype(F32)).astype(BF16)
    return hi, mid, lo


def hot(count, row):
    return (lax.broadcasted_iota(jnp.int32, (count, CAPACITY), 0) == row).astype(F32).astype(BF16)


def ends():
    block, slab = lax.axis_index("blocks"), lax.axis_index("span")
    last_block = block == lax.axis_size("blocks") - 1
    last_slab = slab == lax.axis_size("span") - 1
    return block == 0, last_block, slab == 0, last_slab


def unless(flag):
    return jnp.where(flag, 0.0, 1.0).astype(F32)


def rolled(x, by):
    by = by % x.shape[-1]
    return pltpu.roll(x, by, x.ndim - 1) if by else x


def pack_sides(field, base, rt, lf, keep_rt, keep_lf):
    slot = lax.broadcasted_iota(jnp.int32, (NJ, 128), 1) // 16
    groups = field.shape[0] // 8

    def one(g, carry):
        right = jnp.zeros((NJ, 128), F32)
        left = jnp.zeros((NJ, 128), F32)
        for q in range(8):
            plane = g * 8 + q
            right = jnp.where(slot == q, rolled(field[plane, :, 128:256], 16 * q + 16), right)
            left = jnp.where(slot == q, rolled(field[plane, :, 0:128], 16 * q), left)
        rt[base + g] = right * keep_rt
        lf[base + g] = left * keep_lf
        return carry

    lax.fori_loop(0, groups, one, 0)
    return base + groups


def load(sems, *pairs):
    copies = [pltpu.make_async_copy(src, dst, sems.at[n]) for n, (src, dst) in enumerate(pairs)]
    for c in copies:
        c.start()
    for c in copies:
        c.wait()


def pack_warp_kernel(prior_hbm, inv_hbm, up, dn, prior, inv, sems):
    first_block, last_block, _, _ = ends()
    load(sems, *[(prior_hbm.at[16 * v : 16 * v + 16], prior.at[16 * v : 16 * v + 16]) for v in range(3)], (inv_hbm, inv))
    keep_up, keep_dn = unless(last_block), unless(first_block)
    for v in range(3):
        up[15 * v : 15 * v + 15] = prior[16 * v + 1 : 16 * v + 16, 24:32, :] * keep_up
        dn[15 * v : 15 * v + 15] = prior[16 * v + 1 : 16 * v + 16, 0:8, :] * keep_dn
    up[45:59] = inv[1:15, 24:32, :] * keep_up
    dn[45:59] = inv[1:15, 0:8, :] * keep_dn
    for n in range(45):
        p = 16 * (n // 15) + n % 15 + 1
        up[59 + n // 8, n % 8 : n % 8 + 1, :] = prior[p, 23:24, :] * keep_up
        dn[59 + n // 8, n % 8 : n % 8 + 1, :] = prior[p, 8:9, :] * keep_dn


def pack_rest_kernel(prior_hbm, inv_hbm, off_hbm, coord_hbm, vol_hbm, rt, lf, up, dn, prior, inv, offset, coord, vol, sems):
    first_block, last_block, first_slab, last_slab = ends()
    keep_up, keep_dn = unless(last_block), unless(first_block)
    pairs = [(inv_hbm, inv), (vol_hbm, vol)]
    for v in range(3):
        at = slice(16 * v, 16 * v + 16)
        pairs += [(prior_hbm.at[at], prior.at[at]), (off_hbm.at[at], offset.at[at]), (coord_hbm.at[at], coord.at[at])]
    copies = [pltpu.make_async_copy(src, dst, sems.at[n]) for n, (src, dst) in enumerate(pairs)]
    for c in copies:
        c.start()
    base = 0
    for field, waits in ((prior, (2, 5, 8)), (inv, (0,)), (offset, (3, 6, 9)), (coord, (4, 7, 10)), (vol, (1,))):
        for n in waits:
            copies[n].wait()
        base = pack_sides(field, base, rt, lf, unless(last_slab), unless(first_slab))
    start = 30
    for p in range(48):
        line = slice(p % 8, p % 8 + 1)
        for j in range(5):
            up[5 * (p // 8) + j, line, :] = offset[p, 27 + j : 28 + j, :]
            dn[5 * (p // 8) + j, line, :] = offset[p, j : j + 1, :]
    up[start : start + 15] = vol[0:15, 24:32, :] * keep_up
    dn[start : start + 15] = vol[0:15, 0:8, :] * keep_dn
    start += 15
    low = lax.broadcasted_iota(jnp.int32, (8, NK), 0) < 4
    for m in range(24):
        other = pltpu.roll(coord[m + 24, 24:32, :], 4, 0)
        up[start + m] = jnp.where(low, other, coord[m, 24:32, :]) * keep_up
        other = pltpu.roll(coord[m + 24, 0:8, :], 4, 0)
        dn[start + m] = jnp.where(low, coord[m, 0:8, :], other) * keep_dn


def corner_kernel(from_lf, from_rt, up, dn):
    first_block, last_block, _, _ = ends()
    keep_up, keep_dn = unless(last_block), unless(first_block)
    for s, side in enumerate((from_lf, from_rt)):
        b = 28 * s
        up[b : b + 22] = side[:, 24:32, :] * keep_up
        dn[b : b + 22] = side[:, 0:8, :] * keep_dn
        up[b + 22 : b + 28] = side[0:6, 16:24, :] * keep_up
        dn[b + 22 : b + 28] = side[0:6, 8:16, :] * keep_dn


def route_kernel(
    disp_hbm, blk_hbm, node_hbm, struct_hbm, weight_hbm, send, slots,
    disp, blk, node, struct, weight, table, lhs, rhs, sems,
):
    load(sems, (blk_hbm, blk), (struct_hbm, struct), (disp_hbm, disp), (weight_hbm, weight), (node_hbm, node))
    first = lax.broadcasted_iota(jnp.int32, (32, 128), 0)
    table[...] = jnp.zeros((16, 128), F32)
    for a in range(4):
        table[4 * a : 4 * a + 3, :] = disp[:, 128 * a : 128 * a + 128]
    parts = jnp.concatenate(halves(table[...]), axis=0)
    earlier = (
        lax.broadcasted_iota(jnp.int32, (128, 128), 0) < lax.broadcasted_iota(jnp.int32, (128, 128), 1)
    ).astype(F32).astype(BF16)
    ones = jnp.ones((128, 128), BF16)
    named = [first == blk[c : c + 1, :] for c in range(16)]
    named = [x.astype(F32) for x in named]
    stacked = jnp.concatenate([x.astype(BF16) for x in named], axis=0)
    before = jnp.dot(stacked, earlier, preferred_element_type=F32)
    totals = jnp.dot(stacked, ones, preferred_element_type=F32)
    running = jnp.zeros((32, 128), F32)
    quarter = lax.broadcasted_iota(jnp.int32, (16, 128), 0) // 4
    for c in range(16):
        at = slice(128 * c, 128 * c + 128)
        rank = jnp.sum(named[c] * (before[32 * c : 32 * c + 32] + running), axis=0, keepdims=True)
        running = running + totals[32 * c : 32 * c + 32]
        rhs[:, at] = hot(128, rank.astype(jnp.int32))
        s = struct[c : c + 1, :]
        high, low = s // 128, s % 128
        got = jnp.dot(parts, hot(128, low), preferred_element_type=F32)
        got = got[0:16] + got[16:32] + got[32:48]
        got = jnp.where(quarter == high, got, 0.0)
        got = got[0:8] + got[8:16]
        got = got[0:4] + got[4:8]
        w = weight[c : c + 1, :]
        moved = halves(got[0:3] * w)
        wparts = halves(w)
        n = node[c : c + 1, :]
        rows = [part[v : v + 1] for v in range(3) for part in moved]
        rows += [(n // 256).astype(F32).astype(BF16), (n % 256).astype(F32).astype(BF16)]
        rows += list(wparts)
        rows += [high.astype(F32).astype(BF16), low.astype(F32).astype(BF16)]
        mine = named[c].astype(BF16)
        for p, row in enumerate(rows):
            lhs[32 * p : 32 * p + 32, at] = mine * row
    out = lax.dot_general(lhs[...], rhs[...], NT, preferred_element_type=F32)
    row = lambda p: out[32 * p : 32 * p + 32]
    payload = [row(3 * v) + row(3 * v + 1) + row(3 * v + 2) for v in range(3)]
    payload.append(row(9) * 256.0 + row(10))
    slots[0] = row(11) + row(12) + row(13)
    slots[1] = row(14) * 128.0 + row(15)
    for p, x in enumerate(payload):
        for g in range(32):
            line = x[g : g + 1]
            send[g, 4 + p : 5 + p, :] = line
            if g < 31:
                send[g + 1, p : p + 1, :] = line
            if g > 0:
                send[g - 1, 8 + p : 9 + p, :] = line
    send[0, 0:4, :] = jnp.zeros((4, 128), F32)
    send[31, 8:12, :] = jnp.zeros((4, 128), F32)


def surface_kernel(got, surf, rt, lf, lhs, rhs, lhs_lo, rhs_lo, lhs_up, rhs_up):
    _, _, first_slab, last_slab = ends()
    for s in range(32):
        at = slice(128 * s, 128 * s + 128)
        for kind, (left, right, count, shift) in enumerate(
            ((lhs_lo, rhs_lo, 16, 16), (lhs, rhs, 32, 0), (lhs_up, rhs_up, 16, 0))
        ):
            n = got[s, 4 * kind + 3 : 4 * kind + 4, :].astype(jnp.int32)
            right[:, at] = hot(256, n % 256)
            rows = hot(count, n // 256 - shift)
            parts = halves(got[s, 4 * kind : 4 * kind + 3, :])
            for v in range(3):
                for h in range(3):
                    line = (3 * v + h) * count
                    left[line : line + count, at] = rows * parts[h][v : v + 1]
    for left, right, count, base in ((lhs_lo, rhs_lo, 16, 0), (lhs, rhs, 32, 16), (lhs_up, rhs_up, 16, 48)):
        out = lax.dot_general(left[...], right[...], NT, preferred_element_type=F32)
        for v in range(3):
            b = 3 * v * count
            surf[v, base : base + count, :] = (
                out[b : b + count] + out[b + count : b + 2 * count] + out[b + 2 * count : b + 3 * count]
            )
    rt[...] = surf[:, :, 128:256] * unless(last_slab)
    lf[...] = surf[:, :, 0:128] * unless(first_slab)


def copier(sems):
    copies = []

    def copy(src, dst):
        c = pltpu.make_async_copy(src, dst, sems.at[len(copies)])
        c.start()
        copies.append(c)

    return copies, copy


def bring(copy, field, ext):
    for lt in range(2):
        copy(field.at[:, :, 128 * lt : 128 * lt + 128], ext.at[:, lt, TOP : TOP + NJ, :])


def bring_rims(copy, up, dn, start, ext, first, count):
    for lt in range(2):
        at = slice(128 * lt, 128 * lt + 128)
        copy(up.at[start : start + count, :, at], ext.at[first : first + count, lt, 8:16, :])
        copy(dn.at[start : start + count, :, at], ext.at[first : first + count, lt, 48:56, :])


def bring_sides(exts, base, lf, rt, cup, cdn):
    side = lax.broadcasted_iota(jnp.int32, (8, 128), 1) < 64
    for ext, deep in exts:
        groups = ext.shape[0] // 8

        def one(g, carry, ext=ext, base=base, deep=deep):
            for q in range(8):
                p = g * 8 + q

                def tile(from_rt, from_lf):
                    return jnp.where(side, rolled(from_rt, -16 * q), rolled(from_lf, 112 - 16 * q))

                for t in range(4):
                    rows = slice(8 * t, 8 * t + 8)
                    ext[p, 2, TOP + 8 * t : TOP + 8 * t + 8, :] = tile(rt[base + g, rows, :], lf[base + g, rows, :])
                ext[p, 2, 8:16, :] = tile(cup[28 + base + g], cup[base + g])
                ext[p, 2, 48:56, :] = tile(cdn[28 + base + g], cdn[base + g])
                if deep:
                    ext[p, 2, 0:8, :] = tile(cup[50 + g], cup[22 + g])
                    ext[p, 2, 56:64, :] = tile(cdn[50 + g], cdn[22 + g])
            return carry

        lax.fori_loop(0, groups, one, 0)
        base += groups


def beside(tiles, masks):
    first, last = masks
    out = []
    for n, c in enumerate(tiles):
        before = pltpu.roll(jnp.where(last, tiles[(n + 2) % 3], c), 1, 1)
        after = pltpu.roll(jnp.where(first, tiles[(n + 1) % 3], c), 127, 1)
        out.append(before + after)
    return out


def lane_masks():
    lane = lax.broadcasted_iota(jnp.int32, (8, 128), 1)
    return lane == 0, lane == 127


def warp_kernel(prior, inv, surf, surf_lf, surf_rt, up, dn, lf, rt, cup, cdn, w0, relax, w1, sems):
    copies, copy = copier(sems)
    bring(copy, prior, w0)
    bring(copy, inv, relax)
    for v in range(3):
        bring_rims(copy, up, dn, 15 * v, w0, 16 * v + 1, 15)
    bring_rims(copy, up, dn, 45, relax, 1, 14)
    bring_sides(((w0, True), (relax, False)), 0, lf, rt, cup, cdn)
    for n in range(45):
        p = 16 * (n // 15) + n % 15 + 1
        for lt in range(2):
            at = slice(128 * lt, 128 * lt + 128)
            w0[p, lt, 7:8, :] = up[59 + n // 8, n % 8 : n % 8 + 1, at]
            w0[p, lt, 56:57, :] = dn[59 + n // 8, n % 8 : n % 8 + 1, at]
    for c in copies:
        c.wait()
    wide = lax.broadcasted_iota(jnp.int32, (ROWS, 128), 1) < 64
    for v in range(3):
        for lt in range(2):
            w0[16 * v, lt] = surf[v, :, 128 * lt : 128 * lt + 128]
        w0[16 * v, 2] = jnp.where(wide, surf_rt[v], surf_lf[v])
    masks = lane_masks()

    def sweep(src, dst):
        def component(v, carry):
            b = 16 * v
            for t in TILES:
                r, below, above = (slice(8 * t + d, 8 * t + 8 + d) for d in (0, 1, -1))
                prev = [src[b, n, r, :] for n in range(3)]
                cur = [src[b + 1, n, r, :] for n in range(3)]
                for n in range(3):
                    dst[b, n, r, :] = prev[n]
                for i in range(1, NI - 1):
                    p = b + i
                    nxt = [src[p + 1, n, r, :] for n in range(3)]
                    flat = beside(cur, masks)
                    for n in range(3):
                        total = ((src[p, n, below, :] + src[p, n, above, :]) + flat[n]) + (nxt[n] + prev[n])
                        dst[p, n, r, :] = cur[n] + relax[i, n, r, :] * (total - 6.0 * cur[n])
                    prev, cur = cur, nxt
                for n in range(3):
                    dst[b + NI - 1, n, r, :] = cur[n]
            return carry

        lax.fori_loop(0, 3, component, 0)

    sweep(w0, w1)
    sweep(w1, w0)
    sweep(w0, w1)
    sweep(w1, w0)


def cross(x, y, w):
    return (
        w * (x[1] * y[2] - x[2] * y[1]),
        w * (x[2] * y[0] - x[0] * y[2]),
        w * (x[0] * y[1] - x[1] * y[0]),
    )


def adjoint_kernel(
    offset, coord, vol, field, relax, up, dn, lf, rt, cup, cdn, got,
    warp_out, adj_out, reply,
    s, a, f0, f1, cell, gi, gj, sems,
):
    copies, copy = copier(sems)
    bring(copy, offset, s)
    bring(copy, coord, a)
    bring(copy, vol, cell)
    bring_rims(copy, up, dn, 30, cell, 0, 15)
    bring_rims(copy, up, dn, 45, a, 0, 24)
    for p in range(48):
        line = slice(p % 8, p % 8 + 1)
        for lt in range(2):
            at = slice(128 * lt, 128 * lt + 128)
            s[p, lt, 8:11, :] = jnp.zeros((3, 128), F32)
            s[p, lt, 53:56, :] = jnp.zeros((3, 128), F32)
            for j in range(5):
                s[p, lt, 11 + j : 12 + j, :] = up[5 * (p // 8) + j, line, at]
                s[p, lt, 48 + j : 49 + j, :] = dn[5 * (p // 8) + j, line, at]
    bring_sides(((s, False), (a, False), (cell, False)), 8, lf, rt, cup, cdn)
    for m in range(24):
        for lt in range(2):
            at = slice(128 * lt, 128 * lt + 128)
            a[m + 24, lt, 8:16, :] = pltpu.roll(up[45 + m, :, at], 4, 0)
            a[m + 24, lt, 48:56, :] = pltpu.roll(dn[45 + m, :, at], 4, 0)
    out = [
        pltpu.make_async_copy(
            field.at[:, lt, TOP : TOP + NJ, :], warp_out.at[:, :, 128 * lt : 128 * lt + 128], sems.at[18 + lt]
        )
        for lt in range(2)
    ]
    for c in copies[0:2]:
        c.wait()

    def shape_plane(p, carry):
        s[p, :, 8:56, :] = s[p, :, 8:56, :] + field[p, :, 8:56, :]
        return carry

    lax.fori_loop(0, 48, shape_plane, 0)
    for c in copies[2:]:
        c.wait()
    for c in out:
        c.start()
    _, last_block, _, last_slab = ends()

    @pl.when(last_block)
    def _():
        for i in range(NI):
            for n in range(3):
                cell[i, n, TOP + NJ - 1 : TOP + NJ, :] = jnp.zeros((1, 128), F32)

    @pl.when(last_slab)
    def _():
        lane = lax.broadcasted_iota(jnp.int32, (48, 128), 1)
        for i in range(NI):
            cell[i, 1, 8:56, :] = jnp.where(lane == 127, 0.0, cell[i, 1, 8:56, :])

    gi[...] = jnp.zeros((3, 3, ROWS, 128), F32)
    gj[:, :, 0:8, :] = jnp.zeros((3, 3, 8, 128), F32)
    first, last = masks = lane_masks()

    def grad_plane(i, carry):
        for t in TILES:
            r, below, above = (slice(8 * t + d, 8 * t + 8 + d) for d in (0, 1, -1))
            here = [[s[16 * v + i, n, r, :] for n in range(3)] for v in range(3)]
            along, held = [], []
            for n in range(3):
                ei = [s[16 * v + i + 1, n, r, :] - here[v][n] for v in range(3)]
                ej = [s[16 * v + i, n, below, :] - here[v][n] for v in range(3)]
                ek = [
                    pltpu.roll(jnp.where(first, here[v][(n + 1) % 3], here[v][n]), 127, 1) - here[v][n]
                    for v in range(3)
                ]
                ei[0], ej[1], ek[2] = ei[0] + 1.0, ej[1] + 1.0, ek[2] + 1.0
                w = cell[i, n, r, :]
                new_i, new_j, new_k = cross(ej, ek, w), cross(ek, ei, w), cross(ei, ej, w)
                along.append(new_k)
                held.append([])
                for v in range(3):
                    p = 16 * v + i
                    gj[v, n, r, :] = new_j[v]
                    value = a[p, n, r, :] - new_i[v] + gi[v, n, r, :] - new_j[v]
                    held[n].append(value + gj[v, n, above, :] - new_k[v])
                    gi[v, n, r, :] = new_i[v]
            for n in range(3):
                rel = jnp.where(i > 0, relax[i, n, r, :], 0.0)
                for v in range(3):
                    p = 16 * v + i
                    value = held[n][v] + pltpu.roll(jnp.where(last, along[(n + 2) % 3][v], along[n][v]), 1, 1)
                    a[p, n, r, :] = value
                    f0[p, n, r, :] = rel * value
        return carry

    lax.fori_loop(0, NI - 1, grad_plane, 0)
    for v in range(3):
        p = 16 * v + NI - 1
        a[p, :, 8:56, :] = a[p, :, 8:56, :] + gi[v, :, 8:56, :]

    def sweep(src, dst, final):
        lanes = range(2) if final else range(3)

        def component(v, carry):
            b = 16 * v
            for t in TILES[1:-1] if final else TILES:
                r, below, above = (slice(8 * t + d, 8 * t + 8 + d) for d in (0, 1, -1))
                prev = None
                cur = [src[b + 1, n, r, :] for n in range(3)]
                for n in lanes:
                    a[b, n, r, :] = a[b, n, r, :] + cur[n]
                for i in range(1, NI - 1):
                    p = b + i
                    nxt = [src[p + 1, n, r, :] for n in range(3)] if i < NI - 2 else None
                    flat = beside(cur, masks)
                    for n in lanes:
                        if prev is None:
                            sides = nxt[n]
                        elif nxt is None:
                            sides = prev[n]
                        else:
                            sides = nxt[n] + prev[n]
                        total = ((src[p, n, below, :] + src[p, n, above, :]) + flat[n]) + sides
                        new = a[p, n, r, :] + (total - 6.0 * cur[n])
                        a[p, n, r, :] = new
                        if not final:
                            dst[p, n, r, :] = relax[i, n, r, :] * new
                    prev, cur = cur, nxt
                for n in lanes:
                    a[b + NI - 1, n, r, :] = a[b + NI - 1, n, r, :] + prev[n]
            return carry

        lax.fori_loop(0, 3, component, 0)

    sweep(f0, f1, False)
    sweep(f1, f0, False)
    sweep(f0, f1, False)
    sweep(f1, f0, True)
    copies, copy = copier(sems)
    for lt in range(2):
        copy(a.at[:, lt, TOP : TOP + NJ, :], adj_out.at[:, :, 128 * lt : 128 * lt + 128])

    wall = [jnp.concatenate([a[16 * v, lt, TOP : TOP + NJ, :] for lt in range(2)], axis=1) for v in range(3)]
    table = jnp.concatenate([h for v in range(3) for h in halves(wall[v])], axis=0)
    lines = lax.broadcasted_iota(jnp.int32, (32, 128), 0)
    for q in range(32):
        n = got[q, 7:8, :].astype(jnp.int32)
        picked = jnp.dot(table, hot(256, n % 256), preferred_element_type=F32)
        mine = lines == n // 256
        for v in range(3):
            b = 96 * v
            x = picked[b : b + 32] + picked[b + 32 : b + 64] + picked[b + 64 : b + 96]
            reply[q, v : v + 1, :] = jnp.sum(jnp.where(mine, x, 0.0), axis=0, keepdims=True)
    for c in copies + out:
        c.wait()


def sens_kernel(back, slots, out, lhs, rhs):
    quarter = lax.broadcasted_iota(jnp.int32, (4, 128), 0)
    for g in range(32):
        at = slice(128 * g, 128 * g + 128)
        n = slots[1, g : g + 1, :].astype(jnp.int32)
        high, low = n // 128, n % 128
        rhs[:, at] = hot(128, low)
        value = back[g] * slots[0, g : g + 1, :]
        rows = jnp.concatenate([jnp.where(quarter == high, value[v : v + 1], 0.0) for v in range(3)] + [jnp.zeros((4, 128), F32)], axis=0)
        lhs[:, at] = jnp.concatenate(halves(rows), axis=0)
    total = lax.dot_general(lhs[...], rhs[...], NT, preferred_element_type=F32)
    total = total[0:16] + total[16:32] + total[32:48]
    for v in range(3):
        for q in range(4):
            out[v : v + 1, 128 * q : 128 * q + 128] = total[4 * v + q : 4 * v + q + 1]


def shifted(x, axis, by):
    size = lax.axis_size(axis)
    return lax.ppermute(x, axis, [(i, (i + by) % size) for i in range(size)])


def shape(*dims):
    return jax.ShapeDtypeStruct(dims, F32)


def body(struct_disp, rec_struct, rec_block, rec_node, rec_weight, offset, prior_warp, inv_volume, coord_cot, vol_cot):
    prior = prior_warp.reshape(48, NJ, NK)
    off = offset.reshape(48, NJ, NK)
    coord = coord_cot.reshape(48, NJ, NK)

    hbm = pl.BlockSpec(memory_space=pltpu.HBM)
    light = pl.CostEstimate(flops=1000, bytes_accessed=1000, transcendentals=0)
    records = (struct_disp, *(x.reshape(16, 128) for x in (rec_block, rec_node, rec_struct, rec_weight)))
    lines = [pltpu.VMEM((16, 128), dtype) for dtype in (jnp.int32, jnp.int32, jnp.int32, F32)]
    send, slots = pl.pallas_call(
        route_kernel,
        name="route",
        in_specs=[hbm] * 5,
        out_specs=whole(2),
        out_shape=(shape(32, 12, 128), shape(2, 32, 128)),
        scratch_shapes=[pltpu.VMEM((3, 512), F32)]
        + lines
        + [pltpu.VMEM((16, 128), F32), pltpu.VMEM((512, 2048), BF16), pltpu.VMEM((128, 2048), BF16)]
        + [pltpu.SemaphoreType.DMA((5,))],
        compiler_params=vmem_params(16),
        cost_estimate=light,
    )(*(pltpu.with_memory_space_constraint(x, pltpu.HBM) for x in records))
    got = lax.all_to_all(send, "blocks", split_axis=0, concat_axis=0, tiled=True)

    prior, inv_volume, off, coord, vol_cot = (
        pltpu.with_memory_space_constraint(x, pltpu.HBM) for x in (prior, inv_volume, off, coord, vol_cot)
    )
    three, one = pltpu.VMEM((48, NJ, NK), F32), pltpu.VMEM((16, NJ, NK), F32)
    up1, dn1 = pl.pallas_call(
        pack_warp_kernel,
        name="pack_warp",
        in_specs=[hbm] * 2,
        out_specs=whole(2),
        out_shape=(shape(65, 8, 256), shape(65, 8, 256)),
        scratch_shapes=[three, one, pltpu.SemaphoreType.DMA((4,))],
        compiler_params=vmem_params(5),
        cost_estimate=light,
    )(*(pltpu.with_memory_space_constraint(x, pltpu.HBM) for x in lax.optimization_barrier((prior, inv_volume, send))[:2]))
    tied = lax.optimization_barrier((up1, prior, inv_volume, off, coord, vol_cot))[1:]
    prior_t, inv_t, off_t, coord_t, vol_t = (pltpu.with_memory_space_constraint(x, pltpu.HBM) for x in tied)
    up1 = shifted(up1, "blocks", 1)
    dn1 = shifted(dn1, "blocks", -1)
    rt, lf, up2, dn2 = pl.pallas_call(
        pack_rest_kernel,
        name="pack_rest",
        in_specs=[hbm] * 5,
        out_specs=whole(4),
        out_shape=(shape(22, 32, 128), shape(22, 32, 128), shape(69, 8, 256), shape(69, 8, 256)),
        scratch_shapes=[three, one, three, three, one, pltpu.SemaphoreType.DMA((11,))],
        compiler_params=vmem_params(12),
        cost_estimate=light,
    )(prior_t, inv_t, off_t, coord_t, vol_t)
    from_lf = shifted(rt, "span", 1)
    from_rt = shifted(lf, "span", -1)
    surf, srt, slf = pl.pallas_call(
        surface_kernel,
        name="surface",
        in_specs=whole(1),
        out_specs=whole(3),
        out_shape=(shape(3, 64, 256), shape(3, 64, 128), shape(3, 64, 128)),
        scratch_shapes=[
            pltpu.VMEM((288, 4096), BF16),
            pltpu.VMEM((256, 4096), BF16),
            pltpu.VMEM((144, 4096), BF16),
            pltpu.VMEM((256, 4096), BF16),
            pltpu.VMEM((144, 4096), BF16),
            pltpu.VMEM((256, 4096), BF16),
        ],
        compiler_params=vmem_params(16),
        cost_estimate=light,
    )(got)
    surf_lf = shifted(srt, "span", 1)
    surf_rt = shifted(slf, "span", -1)

    cup, cdn = pl.pallas_call(
        corner_kernel,
        name="corner",
        in_specs=whole(2),
        out_specs=whole(2),
        out_shape=(shape(56, 8, 128), shape(56, 8, 128)),
        compiler_params=vmem_params(4),
        cost_estimate=light,
    )(*lax.optimization_barrier((from_lf, from_rt, surf))[:2])
    cup = shifted(cup, "blocks", 1)
    cdn = shifted(cdn, "blocks", -1)
    up2, dn2, up1, dn1, cup, cdn, surf_lf, surf_rt = lax.optimization_barrier(
        (up2, dn2, up1, dn1, cup, cdn, surf_lf, surf_rt)
    )
    up2 = shifted(up2, "blocks", 1)
    dn2 = shifted(dn2, "blocks", -1)

    big = pltpu.VMEM((48, 3, ROWS, 128), F32)
    field, relax = pl.pallas_call(
        warp_kernel,
        name="warp",
        in_specs=[hbm] * 2 + whole(9),
        out_specs=whole(2),
        out_shape=(shape(48, 3, ROWS, 128), shape(16, 3, ROWS, 128)),
        scratch_shapes=[big, pltpu.SemaphoreType.DMA((20,))],
        compiler_params=vmem_params(16),
        cost_estimate=pl.CostEstimate(flops=60_000_000, bytes_accessed=20_000_000, transcendentals=0),
    )(prior, inv_volume, surf, surf_lf, surf_rt, up1, dn1, from_lf, from_rt, cup, cdn)
    warp_field, adjoint, reply = pl.pallas_call(
        adjoint_kernel,
        name="adjoint",
        in_specs=[hbm] * 3 + whole(9),
        out_specs=[hbm] * 2 + whole(1),
        out_shape=(shape(48, NJ, NK), shape(48, NJ, NK), shape(32, 3, 128)),
        scratch_shapes=[big] * 4
        + [pltpu.VMEM((16, 3, ROWS, 128), F32)]
        + [pltpu.VMEM((3, 3, ROWS, 128), F32)] * 2
        + [pltpu.SemaphoreType.DMA((20,))],
        compiler_params=vmem_params(25),
        cost_estimate=pl.CostEstimate(flops=60_000_000, bytes_accessed=20_000_000, transcendentals=0),
    )(off, coord, vol_cot, field, relax, up2, dn2, from_lf, from_rt, cup, cdn, got)
    back = lax.all_to_all(reply, "blocks", split_axis=0, concat_axis=0, tiled=True)
    struct_sens = pl.pallas_call(
        sens_kernel,
        name="sens",
        in_specs=whole(2),
        out_specs=whole(1)[0],
        out_shape=shape(3, 512),
        scratch_shapes=[pltpu.VMEM((48, 4096), BF16), pltpu.VMEM((128, 4096), BF16)],
        compiler_params=vmem_params(16),
    )(back, slots)
    return (
        warp_field.reshape(3, NI, NJ, NK),
        adjoint.reshape(3, NI, NJ, NK),
        struct_sens,
    )


def solution(mesh):
    placed = (
        P(None, ("blocks", "span")),
        P(("blocks", "span")),
        P(("blocks", "span"), None),
        P(("blocks", "span")),
        P(("blocks", "span")),
        P(None, None, "blocks", "span"),
        P(None, None, "blocks", "span"),
        P(None, "blocks", "span"),
        P(None, None, "blocks", "span"),
        P(None, "blocks", "span"),
    )
    return jax.shard_map(
        body,
        mesh=mesh,
        in_specs=placed,
        out_specs=(
            P(None, None, "blocks", "span"),
            P(None, None, "blocks", "span"),
            P(None, ("blocks", "span")),
        ),
        check_vma=False,
    )
```
